256 devices in a mesh: slab: 128 (over y, x, z_hi, core), grp: 2 (over z_lo).
Axes of the slice: x: 4, y: 4, z: 8 (z_hi: 4, z_lo: 2; z = z_hi * 2 + z_lo), core: 2. Of those that a mesh axis runs over, the one named last changes fastest.
Arguments:
- saturation: float32 [256, 64, 256], P(('slab', 'grp')), may hold values from 0.5 to 3
- inlet_mask: int32 [256, 64, 256], P(('slab', 'grp')), may hold values 0 or 1
- crystal_size: float32 [1048576], P(('slab', 'grp')), may hold values from 0.5 to 2
- crystal_weight: float32 [1048576], P(('slab', 'grp')), may hold values from 0.3 to 3
- crystal_cell: int32 [1048576], P(('slab', 'grp')), may hold values from 0 to 32767
- live_count: int32 [256], P(('slab', 'grp')), may hold values from 1024 to 4096, as said below
- nucleus_cell: int32 [256, 4, 512], P(('slab', 'grp')), may hold values from 0 to 32767
- nucleus_count: int32 [256, 4, 512], P(('slab', 'grp')), may hold values from 1 to 8
- migrant_rows: int32 [256, 2, 512], P(('slab', 'grp')), may hold values from 0 to 4095, as said below
- migrant_count: int32 [256, 2], P(('slab', 'grp')), may hold values from 0 to 512
Outputs:
- saturation_out: float32 [256, 64, 256], P(('slab', 'grp'))
- size_out: float32 [1048576], P(('slab', 'grp'))
- arrivals: float32 [256, 2, 2, 512], P(('slab', 'grp'))
The draws below stay inside these ranges and needn't reach their ends.
Inputs may be any that keep to these rules, and one draw needn't show every extreme that they name: `live_count`: about a quarter of the devices hold exactly 4096 live rows, the others a quarter to a third of that. `migrant_rows`: rows of the device's own parcels below its live count, all distinct; the list toward the lower slab lies in the lower half of the live rows, the other in the upper half.
All inputs are finite; a program needn't handle non-finite values. No bound on the sum of `inlet_mask` on one device may be relied on, other than what follows from the above.
Results may differ from the reference program's by a relative error of at most 0.00007.
Values sent between devices are 32-bit elements; how exact they have to be, the bound alone decides.
A program may use at most 64 MiB of HBM per device.

```python
import math
import jax
import jax.numpy as jnp

PL = 1
NY = 64
NZ = 256
P_SIZE = 4096
MIG = 512
NEV = 512
STEPS = 2
SUBS = 2
DEVS = 256
NX = 256
N_SLAB = 128
N_GRP = 2


def live_counts(key):
    base = jax.random.randint(jax.random.fold_in(key, 11), (DEVS,), P_SIZE // 4, P_SIZE // 3 + 1)
    order = jax.random.permutation(jax.random.fold_in(key, 12), DEVS)
    return jnp.where(order < max(DEVS // 4, 1), P_SIZE, base).astype(jnp.int32)


def draw_live_count(key, part):
    return live_counts(key)


def draw_migrant_rows(key, part):
    totals = live_counts(key)[:, None]
    lower = totals // 2
    upper = totals - lower
    slots = jnp.arange(MIG).astype(jnp.int32)[None, :]
    lower_off = jax.random.randint(jax.random.fold_in(key, 13), (DEVS, MIG), 0, jnp.maximum(lower // MIG, 1))
    upper_off = jax.random.randint(jax.random.fold_in(key, 14), (DEVS, MIG), 0, jnp.maximum(upper // MIG, 1))
    toward_lower = slots * lower // MIG + lower_off
    toward_upper = lower + slots * upper // MIG + upper_off
    toward_upper = jnp.where(slots == MIG - 1, totals - 1, toward_upper)
    return jnp.stack([toward_lower, toward_upper], axis=1).astype(jnp.int32)


def draw_migrant_count(key, part):
    counts = jax.random.randint(jax.random.fold_in(key, 15), (DEVS, 2), 0, MIG + 1)
    order = jax.random.permutation(jax.random.fold_in(key, 16), DEVS)[:, None]
    return jnp.where(order < max(DEVS // 8, 1), MIG, counts).astype(jnp.int32)


def with_ends(array, key, low, top_value):
    spot = [jax.random.randint(jax.random.fold_in(key, axis), (), 0, length) for axis, length in enumerate(array.shape)]
    longest = array.shape.index(max(array.shape))
    beside = spot[:longest] + [(spot[longest] + 1) % array.shape[longest]] + spot[longest + 1:]
    return array.at[tuple(spot)].set(low).at[tuple(beside)].set(top_value)


def block_scale(rng, extent, split, least, largest):
    gain = 1.0
    for position, parts in split:
        steps = jax.random.uniform(jax.random.fold_in(jax.random.fold_in(rng, 6), position), (parts,), jnp.float32, least / len(split), largest / len(split))
        gain = gain * jnp.repeat(jnp.exp(steps), extent[position] // parts).reshape((-1,) + (1,) * (len(extent) - 1 - position))
    return gain


def setup_inputs(seed: int = 0) -> dict:
    seeds = jax.random.split(jax.random.key(seed), 11)
    return {
        "saturation": jnp.clip(0.5 + 2.5 * jax.random.uniform(seeds[0], (NX, NY, NZ), jnp.float32) ** block_scale(seeds[0], (NX, NY, NZ), ((0, 256),), -0.2, 0.2), 0.5, 3.0),
        "inlet_mask": with_ends((jax.random.randint(seeds[1], (NX, NY, NZ), 0, 16) < 1).astype(jnp.int32), jax.random.fold_in(seeds[1], 1), 0, 1),
        "crystal_size": jnp.clip(jnp.exp(math.log(2.0) - 1.3862944 * jax.random.uniform(seeds[2], (DEVS * P_SIZE,), jnp.float32) ** block_scale(seeds[2], (DEVS * P_SIZE,), ((0, 256),), -0.2, 0.2)), 0.5, 2.0),
        "crystal_weight": jnp.clip(jnp.exp(math.log(3.0) - 2.3025851 * jax.random.uniform(seeds[3], (DEVS * P_SIZE,), jnp.float32) ** block_scale(seeds[3], (DEVS * P_SIZE,), ((0, 256),), -0.2, 0.2)), 0.3, 3.0),
        "crystal_cell": with_ends(jax.random.randint(seeds[4], (DEVS * P_SIZE,), 0, N_GRP * PL * NY * NZ), jax.random.fold_in(seeds[4], 1), 0, (N_GRP * PL * NY * NZ) - 1).astype(jnp.int32),
        "live_count": draw_live_count(jax.random.fold_in(seeds[10], 71), 0),
        "nucleus_cell": with_ends(jax.random.randint(seeds[6], (DEVS, STEPS * SUBS, NEV), 0, N_GRP * PL * NY * NZ), jax.random.fold_in(seeds[6], 1), 0, (N_GRP * PL * NY * NZ) - 1).astype(jnp.int32),
        "nucleus_count": with_ends(jax.random.randint(seeds[7], (DEVS, STEPS * SUBS, NEV), 1, 9), jax.random.fold_in(seeds[7], 1), 1, 8).astype(jnp.int32),
        "migrant_rows": draw_migrant_rows(jax.random.fold_in(seeds[10], 71), 0),
        "migrant_count": draw_migrant_count(jax.random.fold_in(seeds[10], 71), 0),
    }


GROWTH = 0.08
VOLUME = 1.0
NUCLEATE = 0.02
DIFFUSE = 0.12
INLET = 4.0


def transport(padded_x, inlet_weight):
    field_mid = padded_x[1:-1]
    padded_yz = jnp.pad(field_mid, ((0, 0), (1, 1), (1, 1)))
    beside = padded_x[2:] + padded_x[:-2]
    beside = beside + padded_yz[:, 2:, 1:-1] + padded_yz[:, :-2, 1:-1]
    beside = beside + padded_yz[:, 1:-1, 2:] + padded_yz[:, 1:-1, :-2]
    field_mid = field_mid + DIFFUSE * (beside - 6.0 * field_mid)
    return field_mid + inlet_weight * (INLET - field_mid)


def reference(saturation, inlet_mask, crystal_size, crystal_weight, crystal_cell, live_count, nucleus_cell, nucleus_count, migrant_rows, migrant_count):
    devices = N_SLAB * N_GRP
    slab_cells = N_GRP * PL * NY * NZ
    slab_of = jnp.arange(devices).astype(jnp.int32) // N_GRP
    offsets = (slab_of * slab_cells).astype(jnp.int32)
    global_cell = (crystal_cell.reshape(devices, P_SIZE) + offsets[:, None]).reshape(-1).astype(jnp.int32)
    row_index = jnp.arange(P_SIZE).astype(jnp.int32)
    active = (row_index[None, :] < live_count[:, None]).astype(jnp.float32).reshape(-1)
    nucleus_global = (nucleus_cell + offsets[:, None, None]).astype(jnp.int32)
    inlet_weight = inlet_mask.astype(jnp.float32)
    crystal = crystal_size
    field = saturation
    for step_index in range(STEPS):
        for sub_index in range(SUBS):
            substep = step_index * SUBS + sub_index
            flat = field.reshape(-1)
            local_sat = flat[global_cell]
            enlarged = crystal + active * GROWTH * jax.nn.softplus(local_sat - 1.0)
            consumed = active * crystal_weight * VOLUME * (enlarged * enlarged * enlarged - crystal * crystal * crystal)
            event_cell = nucleus_global[:, substep, :].reshape(-1)
            event_mass = nucleus_count[:, substep, :].reshape(-1).astype(jnp.float32) * NUCLEATE * jax.nn.softplus(flat[event_cell] - 1.0)
            deposit = jnp.zeros_like(flat).at[global_cell].add(consumed).at[event_cell].add(event_mass)
            field = (flat - deposit).reshape(field.shape)
            crystal = enlarged
        field = transport(jnp.pad(field, ((1, 1), (0, 0), (0, 0))), inlet_weight)
    size_out = active * crystal
    rows = (migrant_rows + (jnp.arange(devices).astype(jnp.int32) * P_SIZE)[:, None, None]).astype(jnp.int32)
    sent = jnp.stack([size_out[rows], crystal_weight[rows]], axis=2)
    slot_live = (jnp.arange(MIG).astype(jnp.int32)[None, None, :] < migrant_count[:, :, None]).astype(jnp.float32)
    sent = (sent * slot_live[:, :, None, :]).reshape(N_SLAB, N_GRP, 2, 2, MIG)
    empty = jnp.zeros_like(sent[:1])
    from_lower = jnp.concatenate([empty, sent[:-1]], axis=0)[:, :, 1]
    from_upper = jnp.concatenate([sent[1:], empty], axis=0)[:, :, 0]
    arrivals = jnp.stack([from_lower, from_upper], axis=2).reshape(devices, 2, 2, MIG)
    return field, size_out, arrivals
```

```python
import jax
import jax.numpy as jnp
from jax import lax
from jax.experimental import pallas as pl
from jax.experimental.pallas import tpu as pltpu
from jax.sharding import PartitionSpec as P

STEPS = 2
SUBS = 2
GROWTH = 0.08
VOLUME = 1.0
NUCLEATE = 0.02
DIFFUSE = 0.12
INLET = 4.0

LANES = 128
ROWS = 8
CHUNK = ROWS * LANES
MESH = pl.DeviceIdType.MESH
F32 = jnp.float32
BF16 = jnp.bfloat16
I32 = jnp.int32


def softplus(x):
    return jnp.maximum(x, 0.0) + jnp.log1p(jnp.exp(-jnp.abs(x)))


def pieces(x, count):
    out = []
    for _ in range(count):
        top = x.astype(BF16)
        out.append(top)
        x = x - top.astype(F32)
    return out


def kernel(
    live_ref,
    mcount_ref,
    sat_hbm,
    inlet_hbm,
    size_hbm,
    weight_hbm,
    cell_hbm,
    ncell_hbm,
    ncount_hbm,
    mrows_hbm,
    field_ref,
    size_ref,
    arrive_ref,
    field,
    inlet,
    sizes,
    weights,
    cells,
    cells_in,
    ncell,
    ncount,
    mrows,
    evcell,
    evcount,
    halo,
    back,
    mig_out,
    mig_in,
    plane_out,
    size_send,
    hot_p,
    hot_t,
    hot_l,
    pair,
    local,
    mass_hi,
    mass_lo,
    mig_hot,
    mig_line,
    local_sem,
    send_sem,
    recv_sem,
):
    ny, nz = field.shape
    plane_cells = ny * nz
    shift = nz.bit_length() - 1
    half = sizes.shape[0] // 2
    parcel_chunks = 2 * half
    s = lax.axis_index("slab")
    g = lax.axis_index("grp")
    slabs = lax.axis_size("slab")
    up = (lax.rem(s + 1, slabs), g)
    down = (lax.rem(s + slabs - 1, slabs), g)
    partner = (s, 1 - g)
    other = (lax.rem(s + slabs + 2 * g - 1, slabs), 1 - g)

    barrier = pltpu.get_barrier_semaphore()
    for peer in (partner, other, up, down):
        pl.semaphore_signal(barrier, inc=1, device_id=peer, device_id_type=MESH)

    loads = []
    for index, (source, target) in enumerate(
        (
            (cell_hbm, cells_in),
            (sat_hbm.at[0], field),
            (size_hbm, sizes.at[pl.ds(0, half)]),
            (weight_hbm, weights.at[pl.ds(0, half)]),
            (ncell_hbm.at[0], ncell.at[0]),
            (ncount_hbm.at[0], ncount.at[0]),
            (inlet_hbm.at[0], inlet),
            (mrows_hbm.at[0], mrows),
        )
    ):
        copy = pltpu.make_async_copy(source, target, local_sem.at[index])
        copy.start()
        loads.append(copy)

    def remote(index, source, target, peer):
        copy = pltpu.make_async_remote_copy(
            src_ref=source,
            dst_ref=target,
            send_sem=send_sem.at[index],
            recv_sem=recv_sem.at[index],
            device_id=peer,
            device_id_type=MESH,
        )
        copy.start()
        return copy

    loads[0].wait()
    live = live_ref[0]
    row_of = (
        lax.broadcasted_iota(I32, (half, ROWS, LANES), 0) * CHUNK
        + lax.broadcasted_iota(I32, (half, ROWS, LANES), 1) * LANES
        + lax.broadcasted_iota(I32, (half, ROWS, LANES), 2)
    )
    is_live = row_of < live
    cells_in[...] = jnp.where(is_live, cells_in[...], -1)
    cells[pl.ds(0, half)] = cells_in[...]

    pl.semaphore_wait(barrier, 4)
    entry = [
        remote(0, cells_in, cells.at[pl.ds(half, half)], partner),
        remote(1, size_hbm, sizes.at[pl.ds(half, half)], partner),
        remote(2, weight_hbm, weights.at[pl.ds(half, half)], partner),
        remote(3, ncell_hbm.at[0], ncell.at[1], partner),
        remote(4, ncount_hbm.at[0], ncount.at[1], partner),
    ]

    base = g * plane_cells
    down_nz = lax.broadcasted_iota(I32, (nz, LANES), 0)
    down_ny = lax.broadcasted_iota(I32, (ny, LANES), 0)
    along_nz = lax.broadcasted_iota(I32, (LANES, nz), 1)

    def build(chunk, tile):
        cell = tile - base
        place = cell & (nz - 1)
        line = cell >> shift
        turned = jnp.transpose(place)
        for j in range(ROWS):
            columns = pl.ds(LANES * j, LANES)
            hot_p[chunk, :, columns] = jnp.where(
                down_nz == place[j : j + 1, :], 1.0, 0.0
            ).astype(BF16)
            hot_l[chunk, :, columns] = jnp.where(
                down_ny == line[j : j + 1, :], 1.0, 0.0
            ).astype(BF16)
            hot_t[chunk, columns, :] = jnp.where(
                along_nz == jnp.broadcast_to(turned[:, j : j + 1], (LANES, nz)),
                1.0,
                0.0,
            ).astype(BF16)

    def build_parcels(first, last):
        def body(chunk, carry):
            build(chunk, cells[chunk])
            return carry

        lax.fori_loop(first, last, body, 0)

    def build_events(sub):
        rows = ROWS // 2
        for side in range(2):
            for j in range(rows):
                columns = pl.ds(LANES * j, LANES)
                at = pl.ds(side * rows + j, 1)
                evcell[sub, at, :] = ncell[side, pl.ds(sub, 1), columns]
                evcount[sub, at, :] = ncount[side, pl.ds(sub, 1), columns].astype(F32)
        build(parcel_chunks + sub, evcell[sub])

    def split_field():
        top, rest = pieces(field[...], 2)
        pair[pl.ds(0, ny), :] = top
        pair[pl.ds(ny, ny), :] = rest

    def gather(chunk):
        both = jnp.dot(pair[...], hot_p[chunk], preferred_element_type=F32)
        read = (both[:ny] + both[ny:]) * hot_l[chunk].astype(F32)
        flat = jnp.sum(read, axis=0, keepdims=True)
        for j in range(ROWS):
            local[chunk, pl.ds(j, 1), :] = flat[:, LANES * j : LANES * (j + 1)]

    def set_mass(chunk, mass):
        top = mass.astype(BF16).astype(F32)
        mass_hi[chunk] = top
        mass_lo[chunk] = mass - top

    def grow(chunk):
        line = (cells[chunk] - base) >> shift
        here = jnp.where((line >= 0) & (line < ny), 1.0, 0.0)
        size = sizes[chunk]
        grown = size + here * GROWTH * softplus(local[chunk] - 1.0)
        sizes[chunk] = grown
        set_mass(
            chunk,
            here
            * weights[chunk]
            * VOLUME
            * (grown * grown * grown - size * size * size),
        )

    def nucleate(sub):
        chunk = parcel_chunks + sub
        set_mass(chunk, evcount[sub] * NUCLEATE * softplus(local[chunk] - 1.0))

    def scatter(chunk):
        lines = hot_l[chunk]
        tops, rests = [], []
        for j in range(ROWS):
            block = lines[:, LANES * j : LANES * (j + 1)]
            top = jnp.broadcast_to(mass_hi[chunk, pl.ds(j, 1), :], (ny, LANES))
            rest = jnp.broadcast_to(mass_lo[chunk, pl.ds(j, 1), :], (ny, LANES))
            tops.append(block * top.astype(BF16))
            rests.append(block * rest.astype(BF16))
        left = jnp.concatenate(
            [jnp.concatenate(tops, axis=1), jnp.concatenate(rests, axis=1)], axis=0
        )
        return jnp.dot(left, hot_t[chunk], preferred_element_type=F32)

    def substep(sub, parcels, with_events, total):
        chunks = list(parcels)
        for chunk in chunks:
            gather(chunk)
        if with_events:
            gather(parcel_chunks + sub)
        for chunk in chunks:
            grow(chunk)
        if with_events:
            nucleate(sub)
            chunks.append(parcel_chunks + sub)
        return chunks

    def deposit(chunks, total):
        for chunk in chunks:
            total = total + scatter(chunk)
        return total

    def take(total):
        field[...] = field[...] - (total[:ny] + total[ny:])

    lane = lax.broadcasted_iota(I32, (ny, nz), 1)
    line = lax.broadcasted_iota(I32, (ny, nz), 0)

    def mix(step):
        plane = field[...]
        plane_out[step] = plane
        first = remote(5 + 2 * step, plane_out.at[step], halo.at[step, 0], partner)
        second = remote(6 + 2 * step, plane_out.at[step], halo.at[step, 1], other)
        return (first, second)

    def mixed(step, copies):
        plane = field[...]
        beside = jnp.where(line == 0, 0.0, pltpu.roll(plane, 1, 0))
        beside = beside + jnp.where(line == ny - 1, 0.0, pltpu.roll(plane, ny - 1, 0))
        beside = beside + jnp.where(lane == 0, 0.0, pltpu.roll(plane, 1, 1))
        beside = beside + jnp.where(lane == nz - 1, 0.0, pltpu.roll(plane, nz - 1, 1))
        for copy in copies:
            copy.wait_recv()
        at_end = jnp.logical_or(
            jnp.logical_and(s == 0, g == 0), jnp.logical_and(s == slabs - 1, g == 1)
        )
        inside = jnp.where(at_end, 0.0, 1.0)
        beside = beside + halo[step, 0] + halo[step, 1] * inside
        plane = plane + DIFFUSE * (beside - 6.0 * plane)
        return plane + inlet[...].astype(F32) * (INLET - plane)

    own = range(half)
    theirs = range(half, parcel_chunks)
    zero = jnp.zeros((2 * ny, nz), F32)

    build_parcels(0, half)
    for copy in loads[1:]:
        copy.wait()
    split_field()
    total = deposit(substep(0, own, False, None), zero)
    for copy in entry:
        copy.wait_recv()
    build_parcels(half, parcel_chunks)
    build_events(0)
    build_events(1)
    total = deposit(substep(0, theirs, True, None), total)
    take(total)
    split_field()
    every = range(parcel_chunks)
    take(deposit(substep(1, every, True, None), zero))
    planes = list(mix(0))
    build_events(2)
    build_events(3)
    slots = mrows.shape[1]
    down_lanes = lax.broadcasted_iota(I32, (LANES, slots), 0)
    down_rows = lax.broadcasted_iota(I32, (half * ROWS, slots), 0)
    slot = lax.broadcasted_iota(I32, (1, slots), 1)
    for j in range(2):
        rows = mrows[pl.ds(j, 1), :]
        mig_hot[j] = jnp.where(down_lanes == (rows & (LANES - 1)), 1.0, 0.0).astype(
            BF16
        )
        used = slot < mcount_ref[0, j]
        mig_line[j] = jnp.where(
            jnp.logical_and(down_rows == (rows >> 7), used), 1.0, 0.0
        )

    def pick(j, table):
        flat = jnp.concatenate(pieces(table, 3), axis=0)
        both = jnp.dot(flat, mig_hot[j], preferred_element_type=F32)
        count = half * ROWS
        read = both[:count] + both[count : 2 * count] + both[2 * count :]
        return jnp.sum(read * mig_line[j], axis=0, keepdims=True)

    weight_table = weights[pl.ds(0, half)].reshape(half * ROWS, LANES)
    for j in range(2):
        mig_out[j, pl.ds(1, 1), :] = pick(j, weight_table)
    field[...] = mixed(0, planes)
    split_field()
    take(deposit(substep(2, every, True, None), zero))
    split_field()
    chunks = substep(3, every, True, None)
    size_send[...] = sizes[pl.ds(half, half)]
    sent_back = remote(9, size_send, back, partner)
    take(deposit(chunks, zero))
    planes += list(mix(1))
    sent_back.wait_recv()
    own_line = (cells[pl.ds(0, half)] - base) >> shift
    here = jnp.logical_and(own_line >= 0, own_line < ny)
    final = jnp.where(here, sizes[pl.ds(0, half)], back[...])
    final = jnp.where(is_live, final, 0.0)
    size_ref[...] = final
    table = final.reshape(half * ROWS, LANES)
    for j in range(2):
        mig_out[j, pl.ds(0, 1), :] = pick(j, table)
    to_down = remote(10, mig_out.at[0], mig_in.at[1], down)
    to_up = remote(11, mig_out.at[1], mig_in.at[0], up)
    field_ref[0] = mixed(1, planes[2:])
    to_down.wait_recv()
    to_up.wait_recv()
    arrive_ref[0, 0] = mig_in[0] * jnp.where(s == 0, 0.0, 1.0)
    arrive_ref[0, 1] = mig_in[1] * jnp.where(s == slabs - 1, 0.0, 1.0)
    for copy in entry + planes + [sent_back, to_down, to_up]:
        copy.wait_send()


def local(
    saturation,
    inlet_mask,
    crystal_size,
    crystal_weight,
    crystal_cell,
    live_count,
    nucleus_cell,
    nucleus_count,
    migrant_rows,
    migrant_count,
):
    _, ny, nz = saturation.shape
    parcels = crystal_size.shape[0]
    half = parcels // CHUNK
    subs, events = nucleus_cell.shape[1:]
    slots = migrant_rows.shape[2]
    tiles = (half, ROWS, LANES)
    chunks = 2 * half + subs
    vmem = pltpu.VMEM
    field, size_out, arrivals = pl.pallas_call(
        kernel,
        out_shape=(
            jax.ShapeDtypeStruct((1, ny, nz), F32),
            jax.ShapeDtypeStruct(tiles, F32),
            jax.ShapeDtypeStruct((1, 2, 2, slots), F32),
        ),
        in_specs=[pl.BlockSpec(memory_space=pltpu.SMEM)] * 2
        + [pl.BlockSpec(memory_space=pl.ANY)] * 8,
        out_specs=(pl.BlockSpec(memory_space=vmem),) * 3,
        scratch_shapes=[
            vmem((ny, nz), F32),
            vmem((ny, nz), I32),
            vmem((2 * half, ROWS, LANES), F32),
            vmem((2 * half, ROWS, LANES), F32),
            vmem((2 * half, ROWS, LANES), I32),
            vmem(tiles, I32),
            vmem((2, subs, events), I32),
            vmem((2, subs, events), I32),
            vmem((2, slots), I32),
            vmem((subs, ROWS, LANES), I32),
            vmem((subs, ROWS, LANES), F32),
            vmem((STEPS, 2, ny, nz), F32),
            vmem(tiles, F32),
            vmem((2, 2, slots), F32),
            vmem((2, 2, slots), F32),
            vmem((STEPS, ny, nz), F32),
            vmem(tiles, F32),
            vmem((chunks, nz, CHUNK), BF16),
            vmem((chunks, CHUNK, nz), BF16),
            vmem((chunks, ny, CHUNK), BF16),
            vmem((2 * ny, nz), BF16),
            vmem((chunks, ROWS, LANES), F32),
            vmem((chunks, ROWS, LANES), F32),
            vmem((chunks, ROWS, LANES), F32),
            vmem((2, LANES, slots), BF16),
            vmem((2, half * ROWS, slots), F32),
            pltpu.SemaphoreType.DMA((8,)),
            pltpu.SemaphoreType.DMA((12,)),
            pltpu.SemaphoreType.DMA((12,)),
        ],
        compiler_params=pltpu.CompilerParams(
            collective_id=0,
            has_side_effects=True,
            vmem_limit_bytes=48 * 1024 * 1024,
        ),
        name="mixer",
    )(
        live_count,
        migrant_count,
        saturation,
        inlet_mask,
        crystal_size.reshape(tiles),
        crystal_weight.reshape(tiles),
        crystal_cell.reshape(tiles),
        nucleus_cell,
        nucleus_count,
        migrant_rows,
    )
    return (field, size_out.reshape(parcels), arrivals)


def solution(mesh):
    rows = P(("slab", "grp"))
    return jax.shard_map(
        local,
        mesh=mesh,
        in_specs=(rows,) * 10,
        out_specs=(rows,) * 3,
        check_vma=False,
    )
```

```python
import jax
import jax.numpy as jnp
from jax import lax
from jax.experimental import pallas as pl
from jax.experimental.pallas import tpu as pltpu
from jax.sharding import PartitionSpec as P

STEPS = 2
SUBS = 2
GROWTH = 0.08
VOLUME = 1.0
NUCLEATE = 0.02
DIFFUSE = 0.12
INLET = 4.0

LANES = 128
ROWS = 8
CHUNK = ROWS * LANES
MESH = pl.DeviceIdType.MESH
F32 = jnp.float32
BF16 = jnp.bfloat16
I32 = jnp.int32


def softplus(x):
    return jnp.maximum(x, 0.0) + jnp.log1p(jnp.exp(-jnp.abs(x)))


def pieces(x, count):
    out = []
    for _ in range(count):
        top = x.astype(BF16)
        out.append(top)
        x = x - top.astype(F32)
    return out


def kernel(
    live_ref,
    mcount_hbm,
    sat_hbm,
    inlet_hbm,
    size_hbm,
    weight_hbm,
    cell_hbm,
    ncell_hbm,
    ncount_hbm,
    mrows_hbm,
    field_ref,
    size_ref,
    arrive_ref,
    mcount_ref,
    field,
    inlet,
    sizes,
    weights,
    cells,
    cells_in,
    ncell,
    ncount,
    mrows,
    evcell,
    evcount,
    halo,
    back,
    mig_size,
    mig_weight,
    got_size,
    got_weight,
    plane_out,
    size_send,
    hot_p,
    hot_t,
    hot_l,
    pair,
    local,
    mass_hi,
    mass_lo,
    mig_hot,
    mig_line,
    local_sem,
    send_sem,
    recv_sem,
):
    ny, nz = field.shape
    plane_cells = ny * nz
    shift = nz.bit_length() - 1
    half = sizes.shape[0] // 2
    parcel_chunks = 2 * half
    s = lax.axis_index("slab")
    g = lax.axis_index("grp")
    slabs = lax.axis_size("slab")
    has_down = s > 0
    has_up = s < slabs - 1
    partner = (s, 1 - g)
    other = (s + 2 * g - 1, 1 - g)
    has_other = jnp.logical_or(
        jnp.logical_and(g == 0, has_down), jnp.logical_and(g == 1, has_up)
    )
    at_end = jnp.logical_not(has_other)

    barrier = pltpu.get_barrier_semaphore()

    def greet(peer):
        pl.semaphore_signal(barrier, inc=1, device_id=peer, device_id_type=MESH)

    greet(partner)

    @pl.when(has_down)
    def _():
        greet((s - 1, g))
        greet((s - 1, 1 - g))

    @pl.when(has_up)
    def _():
        greet((s + 1, g))
        greet((s + 1, 1 - g))

    loads = []
    for index, (source, target) in enumerate(
        (
            (cell_hbm, cells_in),
            (sat_hbm.at[0], field),
            (size_hbm, sizes.at[pl.ds(0, half)]),
            (weight_hbm, weights.at[pl.ds(0, half)]),
            (ncell_hbm.at[0], ncell.at[0]),
            (ncount_hbm.at[0], ncount.at[0]),
            (inlet_hbm.at[0], inlet),
            (mrows_hbm.at[0], mrows.at[0]),
            (mcount_hbm.at[0], mcount_ref.at[0]),
        )
    ):
        copy = pltpu.make_async_copy(source, target, local_sem.at[index])
        copy.start()
        loads.append(copy)

    def when(condition, action):
        if condition is None:
            action()
        else:
            pl.when(condition)(action)

    def remote(index, source, target, peer, sends=None):
        copy = pltpu.make_async_remote_copy(
            src_ref=source,
            dst_ref=target,
            send_sem=send_sem.at[index],
            recv_sem=recv_sem.at[index],
            device_id=peer,
            device_id_type=MESH,
        )
        when(sends, copy.start)
        return copy

    loads[0].wait()
    live = live_ref[0]
    row_of = (
        lax.broadcasted_iota(I32, (half, ROWS, LANES), 0) * CHUNK
        + lax.broadcasted_iota(I32, (half, ROWS, LANES), 1) * LANES
        + lax.broadcasted_iota(I32, (half, ROWS, LANES), 2)
    )
    is_live = row_of < live
    cells_in[...] = jnp.where(is_live, cells_in[...], -1)
    cells[pl.ds(0, half)] = cells_in[...]

    base = g * plane_cells
    down_nz = lax.broadcasted_iota(I32, (nz, LANES), 0)
    down_ny = lax.broadcasted_iota(I32, (ny, LANES), 0)
    along_nz = lax.broadcasted_iota(I32, (LANES, nz), 1)

    def build(chunk, tile):
        cell = tile - base
        place = cell & (nz - 1)
        line = cell >> shift
        turned = jnp.transpose(place)
        for j in range(ROWS):
            columns = pl.ds(LANES * j, LANES)
            hot_p[chunk, :, columns] = jnp.where(
                down_nz == place[j : j + 1, :], 1.0, 0.0
            ).astype(BF16)
            hot_l[chunk, :, columns] = jnp.where(
                down_ny == line[j : j + 1, :], 1.0, 0.0
            ).astype(BF16)
            hot_t[chunk, columns, :] = jnp.where(
                along_nz == jnp.broadcast_to(turned[:, j : j + 1], (LANES, nz)),
                1.0,
                0.0,
            ).astype(BF16)

    def build_parcels(first, last):
        def body(chunk, carry):
            build(chunk, cells[chunk])
            return carry

        lax.fori_loop(first, last, body, 0)

    def build_events(sub):
        rows = ROWS // 2
        for side in range(2):
            for j in range(rows):
                columns = pl.ds(LANES * j, LANES)
                at = pl.ds(side * rows + j, 1)
                evcell[sub, at, :] = ncell[side, pl.ds(sub, 1), columns]
                evcount[sub, at, :] = ncount[side, pl.ds(sub, 1), columns].astype(F32)
        build(parcel_chunks + sub, evcell[sub])

    def split_field():
        top, rest = pieces(field[...], 2)
        pair[pl.ds(0, ny), :] = top
        pair[pl.ds(ny, ny), :] = rest

    def gather(chunk):
        both = jnp.dot(pair[...], hot_p[chunk], preferred_element_type=F32)
        read = (both[:ny] + both[ny:]) * hot_l[chunk].astype(F32)
        flat = jnp.sum(read, axis=0, keepdims=True)
        for j in range(ROWS):
            local[chunk, pl.ds(j, 1), :] = flat[:, LANES * j : LANES * (j + 1)]

    def set_mass(chunk, mass):
        top = mass.astype(BF16).astype(F32)
        mass_hi[chunk] = top
        mass_lo[chunk] = mass - top

    def grow(chunk):
        line = (cells[chunk] - base) >> shift
        here = jnp.where((line >= 0) & (line < ny), 1.0, 0.0)
        size = sizes[chunk]
        grown = size + here * GROWTH * softplus(local[chunk] - 1.0)
        sizes[chunk] = grown
        set_mass(
            chunk,
            here
            * weights[chunk]
            * VOLUME
            * (grown * grown * grown - size * size * size),
        )

    def nucleate(sub):
        chunk = parcel_chunks + sub
        set_mass(chunk, evcount[sub] * NUCLEATE * softplus(local[chunk] - 1.0))

    def scatter(chunk):
        lines = hot_l[chunk]
        tops, rests = [], []
        for j in range(ROWS):
            block = lines[:, LANES * j : LANES * (j + 1)]
            top = jnp.broadcast_to(mass_hi[chunk, pl.ds(j, 1), :], (ny, LANES))
            rest = jnp.broadcast_to(mass_lo[chunk, pl.ds(j, 1), :], (ny, LANES))
            tops.append(block * top.astype(BF16))
            rests.append(block * rest.astype(BF16))
        left = jnp.concatenate(
            [jnp.concatenate(tops, axis=1), jnp.concatenate(rests, axis=1)], axis=0
        )
        return jnp.dot(left, hot_t[chunk], preferred_element_type=F32)

    def substep(sub, parcels, with_events, total):
        chunks = list(parcels)
        for chunk in chunks:
            gather(chunk)
        if with_events:
            gather(parcel_chunks + sub)
        for chunk in chunks:
            grow(chunk)
        if with_events:
            nucleate(sub)
            chunks.append(parcel_chunks + sub)
        return chunks

    def deposit(chunks, total):
        for chunk in chunks:
            total = total + scatter(chunk)
        return total

    def take(total):
        field[...] = field[...] - (total[:ny] + total[ny:])

    lane = lax.broadcasted_iota(I32, (ny, nz), 1)
    line = lax.broadcasted_iota(I32, (ny, nz), 0)

    def mix(step):
        plane_out[step] = field[...]
        source = plane_out.at[step]
        return (
            (remote(5 + 2 * step, source, halo.at[step, 0], partner), None),
            (
                remote(6 + 2 * step, source, halo.at[step, 1], other, has_other),
                has_other,
            ),
        )

    def mixed(step, copies):
        plane = field[...]
        beside = jnp.where(line == 0, 0.0, pltpu.roll(plane, 1, 0))
        beside = beside + jnp.where(line == ny - 1, 0.0, pltpu.roll(plane, ny - 1, 0))
        beside = beside + jnp.where(lane == 0, 0.0, pltpu.roll(plane, 1, 1))
        beside = beside + jnp.where(lane == nz - 1, 0.0, pltpu.roll(plane, nz - 1, 1))
        for copy, condition in copies:
            when(condition, copy.wait_recv)
        beside = beside + halo[step, 0] + halo[step, 1]
        plane = plane + DIFFUSE * (beside - 6.0 * plane)
        return plane + inlet[...].astype(F32) * (INLET - plane)

    own = range(half)
    theirs = range(half, parcel_chunks)
    zero = jnp.zeros((2 * ny, nz), F32)

    @pl.when(at_end)
    def _():
        for step in range(STEPS):
            halo[step, 1] = jnp.zeros((ny, nz), F32)

    def clear(index):
        got_size[index] = jnp.zeros(got_size.shape[1:], F32)
        got_weight[index] = jnp.zeros(got_weight.shape[1:], F32)

    pl.when(jnp.logical_not(has_down))(lambda: clear(0))
    pl.when(jnp.logical_not(has_up))(lambda: clear(1))

    build_parcels(0, half)
    pl.semaphore_wait(
        barrier, 1 + 2 * has_down.astype(I32) + 2 * has_up.astype(I32)
    )
    theirs = pl.ds(half, half)
    entry = [
        remote(0, cells_in, cells.at[theirs], partner),
        remote(1, size_hbm, sizes.at[theirs], partner),
        remote(2, weight_hbm, weights.at[theirs], partner),
        remote(3, ncell_hbm.at[0], ncell.at[1], partner),
        remote(4, ncount_hbm.at[0], ncount.at[1], partner),
        remote(9, mrows_hbm.at[0], mrows.at[1], partner),
    ]
    for copy in loads[1:]:
        copy.wait()
    split_field()
    total = deposit(substep(0, own, False, None), zero)
    for copy in entry:
        copy.wait_recv()
    build_parcels(half, parcel_chunks)
    build_events(0)
    build_events(1)
    total = deposit(substep(0, range(half, parcel_chunks), True, None), total)
    take(total)
    split_field()
    every = range(parcel_chunks)
    take(deposit(substep(1, every, True, None), zero))
    planes = mix(0)
    slots = mrows.shape[2]
    rows_of = half * ROWS
    down_lanes = lax.broadcasted_iota(I32, (LANES, slots), 0)
    down_rows = lax.broadcasted_iota(I32, (rows_of, slots), 0)
    slot = lax.broadcasted_iota(I32, (1, slots), 1)
    for side in range(2):
        for j in range(2):
            rows = mrows[side, pl.ds(j, 1), :]
            mig_hot[side, j] = jnp.where(
                down_lanes == (rows & (LANES - 1)), 1.0, 0.0
            ).astype(BF16)
            mig_line[side, j] = jnp.where(down_rows == (rows >> 7), 1.0, 0.0)

    def pick(side, j, flat):
        both = jnp.dot(flat, mig_hot[side, j], preferred_element_type=F32)
        read = both[:rows_of] + both[rows_of : 2 * rows_of] + both[2 * rows_of :]
        return jnp.sum(read * mig_line[side, j], axis=0, keepdims=True)

    def flat_pieces(table):
        return jnp.concatenate(pieces(table.reshape(rows_of, LANES), 3), axis=0)

    flat = flat_pieces(weights[pl.ds(0, half)])
    for j in range(2):
        used = jnp.where(slot < mcount_ref[0, j], 1.0, 0.0)
        mig_weight[j, pl.ds(0, 1), :] = used
        mig_weight[j, pl.ds(1, 1), :] = pick(0, j, flat) * used
    last = [
        (remote(10, mig_weight.at[0], got_weight.at[1], (s - 1, g), has_down), has_down, has_up),
        (remote(11, mig_weight.at[1], got_weight.at[0], (s + 1, g), has_up), has_up, has_down),
    ]
    build_events(2)
    build_events(3)
    field[...] = mixed(0, planes)
    split_field()
    take(deposit(substep(2, every, True, None), zero))
    split_field()
    chunks = substep(3, every, True, None)
    size_send[...] = sizes[theirs]
    sent_back = remote(12, size_send, back, partner)
    take(deposit(chunks, zero))
    planes = planes + mix(1)
    for side in range(2):
        at = pl.ds(side * half, half)
        mine = (cells[at] - base) >> shift
        here = jnp.logical_and(mine >= 0, mine < ny)
        flat = flat_pieces(jnp.where(here, sizes[at], 0.0))
        to = g if side == 0 else 1 - g
        for j in range(2):
            mig_size[side, j] = pick(side, j, flat)
        last.append(
            (
                remote(13 + 2 * side, mig_size.at[side, 0], got_size.at[1, side], (s - 1, to), has_down),
                has_down,
                has_up,
            )
        )
        last.append(
            (
                remote(14 + 2 * side, mig_size.at[side, 1], got_size.at[0, side], (s + 1, to), has_up),
                has_up,
                has_down,
            )
        )
    sent_back.wait_recv()
    own_line = (cells[pl.ds(0, half)] - base) >> shift
    here = jnp.logical_and(own_line >= 0, own_line < ny)
    final = jnp.where(here, sizes[pl.ds(0, half)], back[...])
    size_ref[...] = jnp.where(is_live, final, 0.0)
    field_ref[0] = mixed(1, planes[2:])
    for copy, _, receives in last:
        when(receives, copy.wait_recv)
    for side in range(2):
        used = got_weight[side, pl.ds(0, 1), :]
        size = got_size[side, 0] + got_size[side, 1]
        arrive_ref[0, side, pl.ds(0, 1), :] = size * used
        arrive_ref[0, side, pl.ds(1, 1), :] = got_weight[side, pl.ds(1, 1), :]
    for copy in entry + [sent_back]:
        copy.wait_send()
    for copy, sends in planes:
        when(sends, copy.wait_send)
    for copy, sends, _ in last:
        when(sends, copy.wait_send)


def store(field_ref, size_ref, arrive_ref, field_out, size_out, arrive_out, sem):
    copies = [
        pltpu.make_async_copy(source, target, sem.at[index])
        for index, (source, target) in enumerate(
            ((field_ref, field_out), (size_ref, size_out), (arrive_ref, arrive_out))
        )
    ]
    for copy in copies:
        copy.start()
    for copy in copies:
        copy.wait()


def local(
    saturation,
    inlet_mask,
    crystal_size,
    crystal_weight,
    crystal_cell,
    live_count,
    nucleus_cell,
    nucleus_count,
    migrant_rows,
    migrant_count,
):
    _, ny, nz = saturation.shape
    parcels = crystal_size.shape[0]
    half = parcels // CHUNK
    subs, events = nucleus_cell.shape[1:]
    slots = migrant_rows.shape[2]
    tiles = (half, ROWS, LANES)
    chunks = 2 * half + subs
    vmem = pltpu.VMEM
    in_vmem = pl.BlockSpec(memory_space=vmem)
    in_hbm = pl.BlockSpec(memory_space=pltpu.HBM)
    shapes = (
        jax.ShapeDtypeStruct((1, ny, nz), F32),
        jax.ShapeDtypeStruct(tiles, F32),
        jax.ShapeDtypeStruct((1, 2, 2, slots), F32),
    )
    results = pl.pallas_call(
        kernel,
        out_shape=shapes,
        in_specs=[pl.BlockSpec(memory_space=pltpu.SMEM)] + [in_hbm] * 9,
        out_specs=(in_vmem,) * 3,
        scratch_shapes=[
            pltpu.SMEM((1, 2), I32),
            vmem((ny, nz), F32),
            vmem((ny, nz), I32),
            vmem((2 * half, ROWS, LANES), F32),
            vmem((2 * half, ROWS, LANES), F32),
            vmem((2 * half, ROWS, LANES), I32),
            vmem(tiles, I32),
            vmem((2, subs, events), I32),
            vmem((2, subs, events), I32),
            vmem((2, 2, slots), I32),
            vmem((subs, ROWS, LANES), I32),
            vmem((subs, ROWS, LANES), F32),
            vmem((STEPS, 2, ny, nz), F32),
            vmem(tiles, F32),
            vmem((2, 2, 1, slots), F32),
            vmem((2, 2, slots), F32),
            vmem((2, 2, 1, slots), F32),
            vmem((2, 2, slots), F32),
            vmem((STEPS, ny, nz), F32),
            vmem(tiles, F32),
            vmem((chunks, nz, CHUNK), BF16),
            vmem((chunks, CHUNK, nz), BF16),
            vmem((chunks, ny, CHUNK), BF16),
            vmem((2 * ny, nz), BF16),
            vmem((chunks, ROWS, LANES), F32),
            vmem((chunks, ROWS, LANES), F32),
            vmem((chunks, ROWS, LANES), F32),
            vmem((2, 2, LANES, slots), BF16),
            vmem((2, 2, half * ROWS, slots), F32),
            pltpu.SemaphoreType.DMA((9,)),
            pltpu.SemaphoreType.DMA((17,)),
            pltpu.SemaphoreType.DMA((17,)),
        ],
        compiler_params=pltpu.CompilerParams(
            collective_id=0,
            has_side_effects=True,
            vmem_limit_bytes=32 * 1024 * 1024,
        ),
        name="mixer",
    )(
        live_count,
        *(
            pltpu.with_memory_space_constraint(operand, pltpu.HBM)
            for operand in (
                migrant_count,
                saturation,
                inlet_mask,
                crystal_size.reshape(tiles),
                crystal_weight.reshape(tiles),
                crystal_cell.reshape(tiles),
                nucleus_cell,
                nucleus_count,
                migrant_rows,
            )
        )
    )
    field, size_out, arrivals = pl.pallas_call(
        store,
        out_shape=shapes,
        in_specs=[pl.BlockSpec(memory_space=pl.ANY)] * 3,
        out_specs=(in_hbm,) * 3,
        scratch_shapes=[pltpu.SemaphoreType.DMA((3,))],
        name="store",
    )(*(pltpu.with_memory_space_constraint(result, vmem) for result in results))
    return (field, size_out.reshape(parcels), arrivals)


def solution(mesh):
    rows = P(("slab", "grp"))
    return jax.shard_map(
        local,
        mesh=mesh,
        in_specs=(rows,) * 10,
        out_specs=(rows,) * 3,
        check_vma=False,
    )
```

```python
import jax
import jax.numpy as jnp
from jax import lax
from jax.experimental import pallas as pl
from jax.experimental.pallas import tpu as pltpu
from jax.sharding import PartitionSpec as P

STEPS = 2
SUBS = 2
GROWTH = 0.08
VOLUME = 1.0
NUCLEATE = 0.02
DIFFUSE = 0.12
INLET = 4.0

LANES = 128
ROWS = 8
CHUNK = ROWS * LANES
MESH = pl.DeviceIdType.MESH
F32 = jnp.float32
BF16 = jnp.bfloat16
I32 = jnp.int32


def softplus(x):
    return jnp.maximum(x, 0.0) + jnp.log1p(jnp.exp(-jnp.abs(x)))


def pieces(x, count):
    out = []
    for _ in range(count):
        top = x.astype(BF16)
        out.append(top)
        x = x - top.astype(F32)
    return out


def when(condition, action):
    if condition is None:
        action()
    else:
        pl.when(condition)(action)


def greet(peer):
    barrier = pltpu.get_barrier_semaphore()
    pl.semaphore_signal(barrier, inc=1, device_id=peer, device_id_type=MESH)


class Hot:
    def __init__(self, base, ny, nz):
        self.base, self.ny, self.nz = base, ny, nz
        self.shift = nz.bit_length() - 1
        self.chunks = {}

    def add(self, first, refs):
        for index in range(refs[0].shape[0]):
            self.chunks[first + index] = (*refs, index)

    def build(self, chunk, tile):
        hot_p, hot_t, hot_l, at = self.chunks[chunk]
        cell = tile - self.base
        place = cell & (self.nz - 1)
        line = cell >> self.shift
        turned = jnp.transpose(place)
        down_nz = lax.broadcasted_iota(I32, (self.nz, LANES), 0)
        down_ny = lax.broadcasted_iota(I32, (self.ny, LANES), 0)
        along_nz = lax.broadcasted_iota(I32, (LANES, self.nz), 1)
        for j in range(ROWS):
            columns = pl.ds(LANES * j, LANES)
            hot_p[at, :, columns] = jnp.where(
                down_nz == place[j : j + 1, :], 1.0, 0.0
            ).astype(BF16)
            hot_l[at, :, columns] = jnp.where(
                down_ny == line[j : j + 1, :], 1.0, 0.0
            ).astype(BF16)
            hot_t[at, columns, :] = jnp.where(
                along_nz == jnp.broadcast_to(turned[:, j : j + 1], (LANES, self.nz)),
                1.0,
                0.0,
            ).astype(BF16)

    def here(self, cells):
        line = (cells - self.base) >> self.shift
        return jnp.logical_and(line >= 0, line < self.ny)

    def gather(self, chunk, pair, local):
        hot_p, _, hot_l, at = self.chunks[chunk]
        ny = self.ny
        both = jnp.dot(pair[...], hot_p[at], preferred_element_type=F32)
        read = (both[:ny] + both[ny:]) * hot_l[at].astype(F32)
        flat = jnp.sum(read, axis=0, keepdims=True)
        for j in range(ROWS):
            local[chunk, pl.ds(j, 1), :] = flat[:, LANES * j : LANES * (j + 1)]

    def scatter(self, chunk, mass):
        _, hot_t, hot_l, at = self.chunks[chunk]
        lines = hot_l[at]
        tops, rests = [], []
        for j in range(ROWS):
            block = lines[:, LANES * j : LANES * (j + 1)]
            row = (self.ny, LANES)
            top = jnp.broadcast_to(mass[chunk, 0, pl.ds(j, 1), :], row)
            rest = jnp.broadcast_to(mass[chunk, 1, pl.ds(j, 1), :], row)
            tops.append(block * top.astype(BF16))
            rests.append(block * rest.astype(BF16))
        left = jnp.concatenate(
            [jnp.concatenate(tops, axis=1), jnp.concatenate(rests, axis=1)], axis=0
        )
        return jnp.dot(left, hot_t[at], preferred_element_type=F32)


def set_mass(mass, chunk, value):
    top = value.astype(BF16).astype(F32)
    mass[chunk, 0] = top
    mass[chunk, 1] = value - top


def deposit(chunks, total, hot, pair, local, mass, weigh):
    for k in range(len(chunks) + 1):
        if k < len(chunks):
            hot.gather(chunks[k], pair, local)
            weigh(chunks[k])
        if k >= 1:
            total = total + hot.scatter(chunks[k - 1], mass)
    return total


def split(plane, pair):
    ny = plane.shape[0]
    top, rest = pieces(plane, 2)
    pair[pl.ds(0, ny), :] = top
    pair[pl.ds(ny, ny), :] = rest


def grower(hot, cells, sizes, weights, local, mass):
    def grow(chunk):
        here = jnp.where(hot.here(cells[chunk]), 1.0, 0.0)
        size = sizes[chunk]
        grown = size + here * GROWTH * softplus(local[chunk] - 1.0)
        sizes[chunk] = grown
        cubes = grown * grown * grown - size * size * size
        set_mass(mass, chunk, here * weights[chunk] * VOLUME * cubes)

    return grow


def event_tiles(sub, ncell, ncount):
    rows = ROWS // 2
    cell, count = [], []
    for side in range(2):
        for j in range(rows):
            columns = slice(LANES * j, LANES * (j + 1))
            cell.append(ncell[side, sub : sub + 1, columns])
            count.append(ncount[side, sub : sub + 1, columns])
    return jnp.concatenate(cell, axis=0), jnp.concatenate(count, axis=0).astype(F32)


def meet(
    live_ref,
    sat_hbm,
    size_hbm,
    weight_hbm,
    cell_hbm,
    ncell_hbm,
    ncount_hbm,
    mrows_hbm,
    field,
    sizes,
    weights,
    cells,
    ncell,
    ncount,
    mrows,
    total,
    hot_p,
    hot_t,
    hot_l,
    cells_in,
    got_cells,
    got_sizes,
    got_weights,
    got_ncell,
    got_ncount,
    got_mrows,
    pair,
    local,
    mass,
    local_sem,
    send_sem,
    recv_sem,
):
    ny, nz = field.shape
    half = cells_in.shape[0]
    s = lax.axis_index("slab")
    g = lax.axis_index("grp")
    partner = (s, 1 - g)
    greet(partner)
    mine = pl.ds(0, half)
    loads = []
    for index, (source, target) in enumerate(
        (
            (cell_hbm, cells_in),
            (sat_hbm.at[0], field),
            (size_hbm, sizes.at[mine]),
            (weight_hbm, weights.at[mine]),
            (ncell_hbm.at[0], ncell.at[0]),
            (ncount_hbm.at[0], ncount.at[0]),
            (mrows_hbm.at[0], mrows.at[0]),
        )
    ):
        copy = pltpu.make_async_copy(source, target, local_sem.at[index])
        copy.start()
        loads.append(copy)

    loads[0].wait()
    live = live_ref[0]
    tiles = cells_in.shape
    row_of = (
        lax.broadcasted_iota(I32, tiles, 0) * CHUNK
        + lax.broadcasted_iota(I32, tiles, 1) * LANES
        + lax.broadcasted_iota(I32, tiles, 2)
    )
    own_cells = jnp.where(row_of < live, cells_in[...], -1)
    cells_in[...] = own_cells
    cells[mine] = own_cells

    pl.semaphore_wait(pltpu.get_barrier_semaphore(), 1)
    entry = []
    for index, (source, target) in enumerate(
        (
            (cells_in, got_cells),
            (ncell_hbm.at[0], got_ncell),
            (size_hbm, got_sizes),
            (weight_hbm, got_weights),
            (ncount_hbm.at[0], got_ncount),
            (mrows_hbm.at[0], got_mrows),
        )
    ):
        copy = pltpu.make_async_remote_copy(
            src_ref=source,
            dst_ref=target,
            send_sem=send_sem.at[index],
            recv_sem=recv_sem.at[index],
            device_id=partner,
            device_id_type=MESH,
        )
        copy.start()
        entry.append(copy)

    hot = Hot(g * (ny * nz), ny, nz)
    hot.add(0, (hot_p, hot_t, hot_l))
    for chunk in range(half):
        hot.build(chunk, cells[chunk])
    for copy in loads[1:]:
        copy.wait()
    split(field[...], pair)
    grow = grower(hot, cells, sizes, weights, local, mass)
    zero = jnp.zeros((2 * ny, nz), F32)
    total[...] = deposit(list(range(half)), zero, hot, pair, local, mass, grow)

    theirs = pl.ds(half, half)
    entry[0].wait_recv()
    cells[theirs] = got_cells[...]
    for chunk in range(half, 2 * half):
        hot.build(chunk, cells[chunk])
    entry[1].wait_recv()
    ncell[1] = got_ncell[...]
    for copy in entry[2:]:
        copy.wait_recv()
    sizes[theirs] = got_sizes[...]
    weights[theirs] = got_weights[...]
    ncount[1] = got_ncount[...]
    mrows[1] = got_mrows[...]
    for sub in range(SUBS):
        hot.build(2 * half + sub, event_tiles(sub, ncell, ncount)[0])
    for copy in entry:
        copy.wait_send()


def run(
    mcount_hbm,
    inlet_hbm,
    field_in,
    sizes_in,
    weights,
    cells,
    ncell,
    ncount,
    mrows,
    total_in,
    hot_p,
    hot_t,
    hot_l,
    field_ref,
    size_ref,
    arrive_ref,
    mcount_ref,
    inlet,
    field,
    sizes,
    halo,
    back,
    mig_size,
    mig_weight,
    got_size,
    got_weight,
    plane_out,
    size_send,
    late_p,
    late_t,
    late_l,
    pair,
    local,
    mass,
    evcount,
    mig_hot,
    mig_line,
    local_sem,
    send_sem,
    recv_sem,
):
    ny, nz = field.shape
    half = back.shape[0]
    parcel_chunks = 2 * half
    s = lax.axis_index("slab")
    g = lax.axis_index("grp")
    slabs = lax.axis_size("slab")
    has_down = s > 0
    has_up = s < slabs - 1
    partner = (s, 1 - g)
    other = (s + 2 * g - 1, 1 - g)
    has_other = jnp.logical_or(
        jnp.logical_and(g == 0, has_down), jnp.logical_and(g == 1, has_up)
    )

    def greet_slab(slab):
        greet((slab, g))
        greet((slab, 1 - g))

    pl.when(has_down)(lambda: greet_slab(s - 1))
    pl.when(has_up)(lambda: greet_slab(s + 1))
    greet(partner)
    loads = []
    for index, (source, target) in enumerate(
        ((mcount_hbm.at[0], mcount_ref.at[0]), (inlet_hbm.at[0], inlet))
    ):
        copy = pltpu.make_async_copy(source, target, local_sem.at[index])
        copy.start()
        loads.append(copy)

    def remote(index, source, target, peer, sends=None):
        copy = pltpu.make_async_remote_copy(
            src_ref=source,
            dst_ref=target,
            send_sem=send_sem.at[index],
            recv_sem=recv_sem.at[index],
            device_id=peer,
            device_id_type=MESH,
        )
        when(sends, copy.start)
        return copy

    hot = Hot(g * (ny * nz), ny, nz)
    hot.add(0, (hot_p, hot_t, hot_l))
    hot.add(hot_p.shape[0], (late_p, late_t, late_l))
    sizes[...] = sizes_in[...]
    grow = grower(hot, cells, sizes, weights, local, mass)

    def weigh(chunk):
        if chunk < parcel_chunks:
            grow(chunk)
        else:
            made = evcount[chunk - parcel_chunks]
            set_mass(mass, chunk, made * NUCLEATE * softplus(local[chunk] - 1.0))

    for sub in range(STEPS * SUBS):
        evcount[sub] = event_tiles(sub, ncell, ncount)[1]

    def substep(plane, chunks, total):
        split(plane, pair)
        total = deposit(chunks, total, hot, pair, local, mass, weigh)
        field[...] = plane - (total[:ny] + total[ny:])

    lane = lax.broadcasted_iota(I32, (ny, nz), 1)
    line = lax.broadcasted_iota(I32, (ny, nz), 0)

    def mix(step):
        plane_out[step] = field[...]
        source = plane_out.at[step]
        first = remote(2 * step, source, halo.at[step, 0], partner)
        second = remote(2 * step + 1, source, halo.at[step, 1], other, has_other)
        return ((first, None), (second, has_other))

    def mixed(step, copies):
        plane = field[...]
        beside = jnp.where(line == 0, 0.0, pltpu.roll(plane, 1, 0))
        beside = beside + jnp.where(line == ny - 1, 0.0, pltpu.roll(plane, ny - 1, 0))
        beside = beside + jnp.where(lane == 0, 0.0, pltpu.roll(plane, 1, 1))
        beside = beside + jnp.where(lane == nz - 1, 0.0, pltpu.roll(plane, nz - 1, 1))
        for copy, condition in copies:
            when(condition, copy.wait_recv)
        beside = beside + halo[step, 0] + halo[step, 1]
        plane = plane + DIFFUSE * (beside - 6.0 * plane)
        return plane + inlet[...].astype(F32) * (INLET - plane)

    @pl.when(jnp.logical_not(has_other))
    def _():
        for step in range(STEPS):
            halo[step, 1] = jnp.zeros((ny, nz), F32)

    def clear(index):
        got_size[index] = jnp.zeros(got_size.shape[1:], F32)
        got_weight[index] = jnp.zeros(got_weight.shape[1:], F32)

    pl.when(jnp.logical_not(has_down))(lambda: clear(0))
    pl.when(jnp.logical_not(has_up))(lambda: clear(1))

    every = list(range(parcel_chunks))
    zero = jnp.zeros((2 * ny, nz), F32)
    substep(field_in[...], every[half:] + [parcel_chunks], total_in[...])
    substep(field[...], every + [parcel_chunks + 1], zero)
    for copy in loads:
        copy.wait()
    pl.semaphore_wait(
        pltpu.get_barrier_semaphore(),
        1 + 2 * has_down.astype(I32) + 2 * has_up.astype(I32),
    )
    planes = mix(0)
    slots = mrows.shape[2]
    rows_of = half * ROWS
    down_lanes = lax.broadcasted_iota(I32, (LANES, slots), 0)
    down_rows = lax.broadcasted_iota(I32, (rows_of, slots), 0)
    slot = lax.broadcasted_iota(I32, (1, slots), 1)
    for side in range(2):
        for j in range(2):
            rows = mrows[side, pl.ds(j, 1), :]
            mig_hot[side, j] = jnp.where(
                down_lanes == (rows & (LANES - 1)), 1.0, 0.0
            ).astype(BF16)
            mig_line[side, j] = jnp.where(down_rows == (rows >> 7), 1.0, 0.0)

    def pick(side, j, flat):
        both = jnp.dot(flat, mig_hot[side, j], preferred_element_type=F32)
        read = both[:rows_of] + both[rows_of : 2 * rows_of] + both[2 * rows_of :]
        return jnp.sum(read * mig_line[side, j], axis=0, keepdims=True)

    def flat_pieces(table):
        return jnp.concatenate(pieces(table.reshape(rows_of, LANES), 3), axis=0)

    flat = flat_pieces(weights[pl.ds(0, half)])
    for j in range(2):
        used = jnp.where(slot < mcount_ref[0, j], 1.0, 0.0)
        mig_weight[j, pl.ds(0, 1), :] = used
        mig_weight[j, pl.ds(1, 1), :] = pick(0, j, flat) * used
    last = []

    def send_both(index, source, target, grp):
        low = remote(index, source[0], target[1], (s - 1, grp), has_down)
        high = remote(index + 1, source[1], target[0], (s + 1, grp), has_up)
        last.append((low, has_down, has_up))
        last.append((high, has_up, has_down))

    send_both(
        4,
        (mig_weight.at[0], mig_weight.at[1]),
        (got_weight.at[0], got_weight.at[1]),
        g,
    )
    for sub in range(SUBS, STEPS * SUBS):
        hot.build(parcel_chunks + sub, event_tiles(sub, ncell, ncount)[0])
    substep(mixed(0, planes), every + [parcel_chunks + 2], zero)
    substep(field[...], every + [parcel_chunks + 3], zero)
    planes = planes + mix(1)
    theirs = pl.ds(half, half)
    size_send[...] = sizes[theirs]
    sent_back = remote(6, size_send, back, partner)
    for side in range(2):
        at = pl.ds(side * half, half)
        flat = flat_pieces(jnp.where(hot.here(cells[at]), sizes[at], 0.0))
        for j in range(2):
            mig_size[side, j] = pick(side, j, flat)
        send_both(
            7 + 2 * side,
            (mig_size.at[side, 0], mig_size.at[side, 1]),
            (got_size.at[0, side], got_size.at[1, side]),
            g if side == 0 else 1 - g,
        )
    sent_back.wait_recv()
    mine = pl.ds(0, half)
    final = jnp.where(hot.here(cells[mine]), sizes[mine], back[...])
    size_ref[...] = jnp.where(cells[mine] >= 0, final, 0.0)
    field_ref[0] = mixed(1, planes[2:])
    for copy, _, receives in last:
        when(receives, copy.wait_recv)
    for side in range(2):
        used = got_weight[side, pl.ds(0, 1), :]
        size = got_size[side, 0] + got_size[side, 1]
        arrive_ref[0, side, pl.ds(0, 1), :] = size * used
        arrive_ref[0, side, pl.ds(1, 1), :] = got_weight[side, pl.ds(1, 1), :]
    sent_back.wait_send()
    for copy, sends in planes:
        when(sends, copy.wait_send)
    for copy, sends, _ in last:
        when(sends, copy.wait_send)


def store(field_ref, size_ref, arrive_ref, field_out, size_out, arrive_out, sem):
    copies = [
        pltpu.make_async_copy(source, target, sem.at[index])
        for index, (source, target) in enumerate(
            ((field_ref, field_out), (size_ref, size_out), (arrive_ref, arrive_out))
        )
    ]
    for copy in copies:
        copy.start()
    for copy in copies:
        copy.wait()


def local(
    saturation,
    inlet_mask,
    crystal_size,
    crystal_weight,
    crystal_cell,
    live_count,
    nucleus_cell,
    nucleus_count,
    migrant_rows,
    migrant_count,
):
    _, ny, nz = saturation.shape
    parcels = crystal_size.shape[0]
    half = parcels // CHUNK
    subs, events = nucleus_cell.shape[1:]
    slots = migrant_rows.shape[2]
    tiles = (half, ROWS, LANES)
    both = (2 * half, ROWS, LANES)
    chunks = 2 * half + subs
    early = 2 * half + SUBS
    vmem = pltpu.VMEM
    dma = pltpu.SemaphoreType.DMA
    in_smem = pl.BlockSpec(memory_space=pltpu.SMEM)
    in_vmem = pl.BlockSpec(memory_space=vmem)
    in_hbm = pl.BlockSpec(memory_space=pltpu.HBM)
    anywhere = pl.BlockSpec(memory_space=pl.ANY)

    def kept(*arrays):
        return [pltpu.with_memory_space_constraint(a, pltpu.HBM) for a in arrays]

    def close(arrays):
        return [pltpu.with_memory_space_constraint(a, vmem) for a in arrays]

    def params(index):
        return pltpu.CompilerParams(
            collective_id=index,
            has_side_effects=True,
            vmem_limit_bytes=20 * 1024 * 1024,
        )

    shape = jax.ShapeDtypeStruct
    met = pl.pallas_call(
        meet,
        out_shape=(
            shape((ny, nz), F32),
            shape(both, F32),
            shape(both, F32),
            shape(both, I32),
            shape((2, subs, events), I32),
            shape((2, subs, events), I32),
            shape((2, 2, slots), I32),
            shape((2 * ny, nz), F32),
            shape((early, nz, CHUNK), BF16),
            shape((early, CHUNK, nz), BF16),
            shape((early, ny, CHUNK), BF16),
        ),
        in_specs=[in_smem] + [in_hbm] * 7,
        out_specs=(in_vmem,) * 11,
        scratch_shapes=[
            vmem(tiles, I32),
            vmem(tiles, I32),
            vmem(tiles, F32),
            vmem(tiles, F32),
            vmem((subs, events), I32),
            vmem((subs, events), I32),
            vmem((2, slots), I32),
            vmem((2 * ny, nz), BF16),
            vmem((chunks, ROWS, LANES), F32),
            vmem((chunks, 2, ROWS, LANES), F32),
            dma((7,)),
            dma((6,)),
            dma((6,)),
        ],
        compiler_params=params(0),
        name="meet",
    )(
        live_count,
        *kept(
            saturation,
            crystal_size.reshape(tiles),
            crystal_weight.reshape(tiles),
            crystal_cell.reshape(tiles),
            nucleus_cell,
            nucleus_count,
            migrant_rows,
        ),
    )
    shapes = (
        shape((1, ny, nz), F32),
        shape(tiles, F32),
        shape((1, 2, 2, slots), F32),
    )
    results = pl.pallas_call(
        run,
        out_shape=shapes,
        in_specs=[in_hbm] * 2 + [in_vmem] * 11,
        out_specs=(in_vmem,) * 3,
        scratch_shapes=[
            pltpu.SMEM((1, 2), I32),
            vmem((ny, nz), I32),
            vmem((ny, nz), F32),
            vmem(both, F32),
            vmem((STEPS, 2, ny, nz), F32),
            vmem(tiles, F32),
            vmem((2, 2, 1, slots), F32),
            vmem((2, 2, slots), F32),
            vmem((2, 2, 1, slots), F32),
            vmem((2, 2, slots), F32),
            vmem((STEPS, ny, nz), F32),
            vmem(tiles, F32),
            vmem((chunks - early, nz, CHUNK), BF16),
            vmem((chunks - early, CHUNK, nz), BF16),
            vmem((chunks - early, ny, CHUNK), BF16),
            vmem((2 * ny, nz), BF16),
            vmem((chunks, ROWS, LANES), F32),
            vmem((chunks, 2, ROWS, LANES), F32),
            vmem((subs, ROWS, LANES), F32),
            vmem((2, 2, LANES, slots), BF16),
            vmem((2, 2, half * ROWS, slots), F32),
            dma((2,)),
            dma((11,)),
            dma((11,)),
        ],
        compiler_params=params(1),
        name="run",
    )(*kept(migrant_count, inlet_mask), *close(met))
    field, size_out, arrivals = pl.pallas_call(
        store,
        out_shape=shapes,
        in_specs=[anywhere] * 3,
        out_specs=(in_hbm,) * 3,
        scratch_shapes=[dma((3,))],
        name="store",
    )(*close(results))
    return (field, size_out.reshape(parcels), arrivals)


def solution(mesh):
    rows = P(("slab", "grp"))
    return jax.shard_map(
        local,
        mesh=mesh,
        in_specs=(rows,) * 10,
        out_specs=(rows,) * 3,
        check_vma=False,
    )
```

```python
import jax
import jax.numpy as jnp
from jax import lax
from jax.experimental import pallas as pl
from jax.experimental.pallas import tpu as pltpu
from jax.sharding import PartitionSpec as P

STEPS = 2
SUBS = 2
GROWTH = 0.08
VOLUME = 1.0
NUCLEATE = 0.02
DIFFUSE = 0.12
INLET = 4.0

LANES = 128
ROWS = 8
CHUNK = ROWS * LANES
EARLY = 1
LAG = 1
MESH = pl.DeviceIdType.MESH
F32 = jnp.float32
BF16 = jnp.bfloat16
I32 = jnp.int32


def softplus(x):
    return jnp.maximum(x, 0.0) + jnp.log1p(jnp.exp(-jnp.abs(x)))


def pieces(x, count):
    out = []
    for _ in range(count):
        top = x.astype(BF16)
        out.append(top)
        x = x - top.astype(F32)
    return out


def when(condition, action):
    if condition is None:
        action()
    else:
        pl.when(condition)(action)


def greet(peer):
    barrier = pltpu.get_barrier_semaphore()
    pl.semaphore_signal(barrier, inc=1, device_id=peer, device_id_type=MESH)


class Hot:
    def __init__(self, base, ny, nz):
        self.base, self.ny, self.nz = base, ny, nz
        self.shift = nz.bit_length() - 1
        self.chunks = {}

    def add(self, first, refs):
        for index in range(refs[0].shape[0]):
            self.chunks[first + index] = (*refs, index)

    def build(self, chunk, tile):
        hot_p, hot_t, hot_l, at = self.chunks[chunk]
        cell = tile - self.base
        place = cell & (self.nz - 1)
        line = cell >> self.shift
        placed, lined = place.astype(F32), line.astype(F32)
        turned = jnp.transpose(placed)

        def iota(shape, dim):
            return lax.broadcasted_iota(I32, shape, dim).astype(F32).astype(BF16)

        down_nz = iota((self.nz, LANES), 0)
        down_ny = iota((self.ny, LANES), 0)
        along_nz = iota((LANES, self.nz), 1)
        one, none = jnp.ones((), BF16), jnp.zeros((), BF16)
        for j in range(ROWS):
            columns = pl.ds(LANES * j, LANES)

            def spread(row, shape):
                return jnp.broadcast_to(row, shape).astype(BF16)

            row = slice(j, j + 1)
            hot_p[at, :, columns] = jnp.where(
                down_nz == spread(placed[row, :], down_nz.shape), one, none
            )
            hot_l[at, :, columns] = jnp.where(
                down_ny == spread(lined[row, :], down_ny.shape), one, none
            )
            hot_t[at, columns, :] = jnp.where(
                along_nz == spread(turned[:, row], along_nz.shape), one, none
            )

    def here(self, cells):
        line = (cells - self.base) >> self.shift
        return jnp.logical_and(line >= 0, line < self.ny)

    def gather(self, chunk, pair, local):
        hot_p, _, hot_l, at = self.chunks[chunk]
        ny = self.ny
        both = jnp.dot(pair[...], hot_p[at], preferred_element_type=F32)
        read = (both[:ny] + both[ny:]) * hot_l[at].astype(F32)
        flat = jnp.sum(read, axis=0, keepdims=True)
        for j in range(ROWS):
            local[chunk, pl.ds(j, 1), :] = flat[:, LANES * j : LANES * (j + 1)]

    def scatter(self, chunk, mass):
        _, hot_t, hot_l, at = self.chunks[chunk]
        lines = hot_l[at]
        tops, rests = [], []
        for j in range(ROWS):
            block = lines[:, LANES * j : LANES * (j + 1)]
            row = (self.ny, LANES)
            top = jnp.broadcast_to(mass[chunk, 0, pl.ds(j, 1), :], row)
            rest = jnp.broadcast_to(mass[chunk, 1, pl.ds(j, 1), :], row)
            tops.append(block * top.astype(BF16))
            rests.append(block * rest.astype(BF16))
        left = jnp.concatenate(
            [jnp.concatenate(tops, axis=1), jnp.concatenate(rests, axis=1)], axis=0
        )
        return jnp.dot(left, hot_t[at], preferred_element_type=F32)


def set_mass(mass, chunk, value):
    top = value.astype(BF16).astype(F32)
    mass[chunk, 0] = top
    mass[chunk, 1] = value - top


def deposit(chunks, total, hot, pair, local, mass, weigh):
    for k in range(len(chunks) + 1):
        if k < len(chunks):
            hot.gather(chunks[k], pair, local)
            weigh(chunks[k])
        if k >= 1:
            total = total + hot.scatter(chunks[k - 1], mass)
    return total


def split(plane, pair):
    ny = plane.shape[0]
    top, rest = pieces(plane, 2)
    pair[pl.ds(0, ny), :] = top
    pair[pl.ds(ny, ny), :] = rest


def grower(hot, cells, sizes, weights, local, mass):
    def grow(chunk):
        here = jnp.where(hot.here(cells[chunk]), 1.0, 0.0)
        size = sizes[chunk]
        grown = size + here * GROWTH * softplus(local[chunk] - 1.0)
        sizes[chunk] = grown
        cubes = grown * grown * grown - size * size * size
        set_mass(mass, chunk, here * weights[chunk] * VOLUME * cubes)

    return grow


def event_tiles(sub, ncell, ncount):
    rows = ROWS // 2
    cell, count = [], []
    for side in range(2):
        for j in range(rows):
            columns = slice(LANES * j, LANES * (j + 1))
            cell.append(ncell[side, sub : sub + 1, columns])
            count.append(ncount[side, sub : sub + 1, columns])
    return jnp.concatenate(cell, axis=0), jnp.concatenate(count, axis=0).astype(F32)


def meet(
    live_ref,
    sat_hbm,
    size_hbm,
    weight_hbm,
    cell_hbm,
    ncell_hbm,
    ncount_hbm,
    mrows_hbm,
    field,
    sizes,
    weights,
    cells,
    ncell,
    ncount,
    mrows,
    total,
    hot_p,
    hot_t,
    hot_l,
    cells_in,
    got_cells,
    got_sizes,
    got_weights,
    got_ncell,
    got_ncount,
    got_mrows,
    pair,
    local,
    mass,
    local_sem,
    send_sem,
    recv_sem,
):
    ny, nz = field.shape
    half = cells_in.shape[0]
    s = lax.axis_index("slab")
    g = lax.axis_index("grp")
    partner = (s, 1 - g)
    greet(partner)
    mine = pl.ds(0, half)
    loads = []
    for index, (source, target) in enumerate(
        (
            (cell_hbm, cells_in),
            (sat_hbm.at[0], field),
            (size_hbm, sizes.at[mine]),
            (weight_hbm, weights.at[mine]),
            (ncell_hbm.at[0], ncell.at[0]),
            (ncount_hbm.at[0], ncount.at[0]),
            (mrows_hbm.at[0], mrows.at[0]),
        )
    ):
        copy = pltpu.make_async_copy(source, target, local_sem.at[index])
        copy.start()
        loads.append(copy)

    loads[0].wait()
    live = live_ref[0]
    tiles = cells_in.shape
    row_of = (
        lax.broadcasted_iota(I32, tiles, 0) * CHUNK
        + lax.broadcasted_iota(I32, tiles, 1) * LANES
        + lax.broadcasted_iota(I32, tiles, 2)
    )
    own_cells = jnp.where(row_of < live, cells_in[...], -1)
    cells_in[...] = own_cells
    cells[mine] = own_cells

    pl.semaphore_wait(pltpu.get_barrier_semaphore(), 1)
    entry = []
    for index, (source, target) in enumerate(
        (
            (cells_in, got_cells),
            (ncell_hbm.at[0], got_ncell),
            (size_hbm, got_sizes),
            (weight_hbm, got_weights),
            (ncount_hbm.at[0], got_ncount),
            (mrows_hbm.at[0], got_mrows),
        )
    ):
        copy = pltpu.make_async_remote_copy(
            src_ref=source,
            dst_ref=target,
            send_sem=send_sem.at[index],
            recv_sem=recv_sem.at[index],
            device_id=partner,
            device_id_type=MESH,
        )
        copy.start()
        entry.append(copy)

    hot = Hot(g * (ny * nz), ny, nz)
    hot.add(0, (hot_p, hot_t, hot_l))
    for chunk in range(half):
        hot.build(chunk, cells[chunk])
    for copy in loads[1:]:
        copy.wait()
    split(field[...], pair)
    grow = grower(hot, cells, sizes, weights, local, mass)
    zero = jnp.zeros((2 * ny, nz), F32)
    total[...] = deposit(list(range(half)), zero, hot, pair, local, mass, grow)

    theirs = pl.ds(half, half)
    entry[0].wait_recv()
    cells[theirs] = got_cells[...]
    for chunk in range(half, 2 * half):
        hot.build(chunk, cells[chunk])
    entry[1].wait_recv()
    ncell[1] = got_ncell[...]
    for copy in entry[2:]:
        copy.wait_recv()
    sizes[theirs] = got_sizes[...]
    weights[theirs] = got_weights[...]
    ncount[1] = got_ncount[...]
    mrows[1] = got_mrows[...]
    for sub in range(SUBS):
        hot.build(2 * half + sub, event_tiles(sub, ncell, ncount)[0])
    for copy in entry:
        copy.wait_send()


def run(
    mcount_hbm,
    inlet_hbm,
    field_in,
    sizes_in,
    weights,
    cells,
    ncell,
    ncount,
    mrows,
    total_in,
    hot_p,
    hot_t,
    hot_l,
    field_ref,
    size_ref,
    arrive_ref,
    mcount_ref,
    inlet,
    field,
    sizes,
    halo,
    back,
    mig_size,
    mig_weight,
    got_size,
    got_weight,
    plane_out,
    size_send,
    late_p,
    late_t,
    late_l,
    pair,
    local,
    mass,
    evcount,
    mig_hot,
    mig_line,
    local_sem,
    send_sem,
    recv_sem,
):
    ny, nz = field.shape
    half = back.shape[0]
    parcel_chunks = 2 * half
    s = lax.axis_index("slab")
    g = lax.axis_index("grp")
    slabs = lax.axis_size("slab")
    has_down = s > 0
    has_up = s < slabs - 1
    partner = (s, 1 - g)
    other = (s + 2 * g - 1, 1 - g)
    has_other = jnp.logical_or(
        jnp.logical_and(g == 0, has_down), jnp.logical_and(g == 1, has_up)
    )

    def greet_slab(slab):
        greet((slab, g))
        greet((slab, 1 - g))

    pl.when(has_down)(lambda: greet_slab(s - 1))
    pl.when(has_up)(lambda: greet_slab(s + 1))
    greet(partner)
    loads = []
    for index, (source, target) in enumerate(
        ((mcount_hbm.at[0], mcount_ref.at[0]), (inlet_hbm.at[0], inlet))
    ):
        copy = pltpu.make_async_copy(source, target, local_sem.at[index])
        copy.start()
        loads.append(copy)

    def remote(index, source, target, peer, sends=None):
        copy = pltpu.make_async_remote_copy(
            src_ref=source,
            dst_ref=target,
            send_sem=send_sem.at[index],
            recv_sem=recv_sem.at[index],
            device_id=peer,
            device_id_type=MESH,
        )
        when(sends, copy.start)
        return copy

    hot = Hot(g * (ny * nz), ny, nz)
    hot.add(0, (hot_p, hot_t, hot_l))
    hot.add(hot_p.shape[0], (late_p, late_t, late_l))
    sizes[...] = sizes_in[...]
    grow = grower(hot, cells, sizes, weights, local, mass)

    def weigh(chunk):
        if chunk < parcel_chunks:
            grow(chunk)
        else:
            made = evcount[chunk - parcel_chunks]
            set_mass(mass, chunk, made * NUCLEATE * softplus(local[chunk] - 1.0))

    for sub in range(STEPS * SUBS):
        evcount[sub] = event_tiles(sub, ncell, ncount)[1]

    def substep(plane, chunks, total):
        split(plane, pair)
        total = deposit(chunks, total, hot, pair, local, mass, weigh)
        field[...] = plane - (total[:ny] + total[ny:])

    lane = lax.broadcasted_iota(I32, (ny, nz), 1)
    line = lax.broadcasted_iota(I32, (ny, nz), 0)

    def mix(step):
        plane_out[step] = field[...]
        source = plane_out.at[step]
        first = remote(2 * step, source, halo.at[step, 0], partner)
        second = remote(2 * step + 1, source, halo.at[step, 1], other, has_other)
        return ((first, None), (second, has_other))

    def mixed(step, copies):
        plane = field[...]
        beside = jnp.where(line == 0, 0.0, pltpu.roll(plane, 1, 0))
        beside = beside + jnp.where(line == ny - 1, 0.0, pltpu.roll(plane, ny - 1, 0))
        beside = beside + jnp.where(lane == 0, 0.0, pltpu.roll(plane, 1, 1))
        beside = beside + jnp.where(lane == nz - 1, 0.0, pltpu.roll(plane, nz - 1, 1))
        for copy, condition in copies:
            when(condition, copy.wait_recv)
        beside = beside + halo[step, 0] + halo[step, 1]
        plane = plane + DIFFUSE * (beside - 6.0 * plane)
        return plane + inlet[...].astype(F32) * (INLET - plane)

    @pl.when(jnp.logical_not(has_other))
    def _():
        for step in range(STEPS):
            halo[step, 1] = jnp.zeros((ny, nz), F32)

    def clear(index):
        got_size[index] = jnp.zeros(got_size.shape[1:], F32)
        got_weight[index] = jnp.zeros(got_weight.shape[1:], F32)

    pl.when(jnp.logical_not(has_down))(lambda: clear(0))
    pl.when(jnp.logical_not(has_up))(lambda: clear(1))

    every = list(range(parcel_chunks))
    zero = jnp.zeros((2 * ny, nz), F32)
    substep(field_in[...], every[half:] + [parcel_chunks], total_in[...])
    substep(field[...], every + [parcel_chunks + 1], zero)
    for copy in loads:
        copy.wait()
    pl.semaphore_wait(
        pltpu.get_barrier_semaphore(),
        1 + 2 * has_down.astype(I32) + 2 * has_up.astype(I32),
    )
    planes = mix(0)
    slots = mrows.shape[2]
    rows_of = half * ROWS
    down_lanes = lax.broadcasted_iota(I32, (LANES, slots), 0)
    down_rows = lax.broadcasted_iota(I32, (rows_of, slots), 0)
    slot = lax.broadcasted_iota(I32, (1, slots), 1)
    for side in range(2):
        for j in range(2):
            rows = mrows[side, pl.ds(j, 1), :]
            mig_hot[side, j] = jnp.where(
                down_lanes == (rows & (LANES - 1)), 1.0, 0.0
            ).astype(BF16)
            mig_line[side, j] = jnp.where(down_rows == (rows >> 7), 1.0, 0.0)

    def pick(side, j, flat):
        both = jnp.dot(flat, mig_hot[side, j], preferred_element_type=F32)
        read = sum(
            both[at : at + rows_of] for at in range(0, flat.shape[0], rows_of)
        )
        return jnp.sum(read * mig_line[side, j], axis=0, keepdims=True)

    def flat_pieces(table, count):
        return jnp.concatenate(pieces(table.reshape(rows_of, LANES), count), axis=0)

    flat = flat_pieces(weights[pl.ds(0, half)], 3)
    for j in range(2):
        used = jnp.where(slot < mcount_ref[0, j], 1.0, 0.0)
        mig_weight[j, pl.ds(0, 1), :] = used
        mig_weight[j, pl.ds(1, 1), :] = pick(0, j, flat) * used
    last = []

    def send_both(index, source, target, grp):
        low = remote(index, source[0], target[1], (s - 1, grp), has_down)
        high = remote(index + 1, source[1], target[0], (s + 1, grp), has_up)
        last.append((low, has_down, has_up))
        last.append((high, has_up, has_down))

    send_both(
        4,
        (mig_weight.at[0], mig_weight.at[1]),
        (got_weight.at[0], got_weight.at[1]),
        g,
    )
    for sub in range(SUBS, STEPS * SUBS):
        hot.build(parcel_chunks + sub, event_tiles(sub, ncell, ncount)[0])
    substep(mixed(0, planes), every + [parcel_chunks + 2], zero)
    plane = field[...]
    split(plane, pair)
    events = parcel_chunks + 3
    total = zero
    done = 0
    for chunk in [events] + every:
        hot.gather(chunk, pair, local)
        weigh(chunk)
        if chunk < events and chunk >= LAG:
            total = total + hot.scatter(chunk - LAG, mass)
            done = chunk - LAG + 1
    for side in range(2):
        at = pl.ds(side * half, half)
        flat = flat_pieces(jnp.where(hot.here(cells[at]), sizes[at], 0.0), 2)
        for j in range(2):
            mig_size[side, j] = pick(side, j, flat)
    rest = every[done:] + [events]
    for chunk in rest[:EARLY]:
        total = total + hot.scatter(chunk, mass)
    for side in range(2):
        send_both(
            7 + 2 * side,
            (mig_size.at[side, 0], mig_size.at[side, 1]),
            (got_size.at[0, side], got_size.at[1, side]),
            g if side == 0 else 1 - g,
        )
    for chunk in rest[EARLY:]:
        total = total + hot.scatter(chunk, mass)
    field[...] = plane - (total[:ny] + total[ny:])
    planes = planes + mix(1)
    theirs = pl.ds(half, half)
    size_send[...] = sizes[theirs]
    sent_back = remote(6, size_send, back, partner)
    sent_back.wait_recv()
    mine = pl.ds(0, half)
    final = jnp.where(hot.here(cells[mine]), sizes[mine], back[...])
    size_ref[...] = jnp.where(cells[mine] >= 0, final, 0.0)
    field_ref[0] = mixed(1, planes[2:])
    for copy, _, receives in last:
        when(receives, copy.wait_recv)
    for side in range(2):
        used = got_weight[side, pl.ds(0, 1), :]
        size = got_size[side, 0] + got_size[side, 1]
        arrive_ref[0, side, pl.ds(0, 1), :] = size * used
        arrive_ref[0, side, pl.ds(1, 1), :] = got_weight[side, pl.ds(1, 1), :]
    sent_back.wait_send()
    for copy, sends in planes:
        when(sends, copy.wait_send)
    for copy, sends, _ in last:
        when(sends, copy.wait_send)


def store(field_ref, size_ref, arrive_ref, field_out, size_out, arrive_out, sem):
    copies = [
        pltpu.make_async_copy(source, target, sem.at[index])
        for index, (source, target) in enumerate(
            ((field_ref, field_out), (size_ref, size_out), (arrive_ref, arrive_out))
        )
    ]
    for copy in copies:
        copy.start()
    for copy in copies:
        copy.wait()


def local(
    saturation,
    inlet_mask,
    crystal_size,
    crystal_weight,
    crystal_cell,
    live_count,
    nucleus_cell,
    nucleus_count,
    migrant_rows,
    migrant_count,
):
    _, ny, nz = saturation.shape
    parcels = crystal_size.shape[0]
    half = parcels // CHUNK
    subs, events = nucleus_cell.shape[1:]
    slots = migrant_rows.shape[2]
    tiles = (half, ROWS, LANES)
    both = (2 * half, ROWS, LANES)
    chunks = 2 * half + subs
    early = 2 * half + SUBS
    vmem = pltpu.VMEM
    dma = pltpu.SemaphoreType.DMA
    in_smem = pl.BlockSpec(memory_space=pltpu.SMEM)
    in_vmem = pl.BlockSpec(memory_space=vmem)
    in_hbm = pl.BlockSpec(memory_space=pltpu.HBM)
    anywhere = pl.BlockSpec(memory_space=pl.ANY)

    def kept(*arrays):
        return [pltpu.with_memory_space_constraint(a, pltpu.HBM) for a in arrays]

    def close(arrays):
        return [pltpu.with_memory_space_constraint(a, vmem) for a in arrays]

    def params(index):
        return pltpu.CompilerParams(
            collective_id=index,
            has_side_effects=True,
            vmem_limit_bytes=20 * 1024 * 1024,
        )

    shape = jax.ShapeDtypeStruct
    met = pl.pallas_call(
        meet,
        out_shape=(
            shape((ny, nz), F32),
            shape(both, F32),
            shape(both, F32),
            shape(both, I32),
            shape((2, subs, events), I32),
            shape((2, subs, events), I32),
            shape((2, 2, slots), I32),
            shape((2 * ny, nz), F32),
            shape((early, nz, CHUNK), BF16),
            shape((early, CHUNK, nz), BF16),
            shape((early, ny, CHUNK), BF16),
        ),
        in_specs=[in_smem] + [in_hbm] * 7,
        out_specs=(in_vmem,) * 11,
        scratch_shapes=[
            vmem(tiles, I32),
            vmem(tiles, I32),
            vmem(tiles, F32),
            vmem(tiles, F32),
            vmem((subs, events), I32),
            vmem((subs, events), I32),
            vmem((2, slots), I32),
            vmem((2 * ny, nz), BF16),
            vmem((chunks, ROWS, LANES), F32),
            vmem((chunks, 2, ROWS, LANES), F32),
            dma((7,)),
            dma((6,)),
            dma((6,)),
        ],
        compiler_params=params(0),
        name="meet",
    )(
        live_count,
        *kept(
            saturation,
            crystal_size.reshape(tiles),
            crystal_weight.reshape(tiles),
            crystal_cell.reshape(tiles),
            nucleus_cell,
            nucleus_count,
            migrant_rows,
        ),
    )
    shapes = (
        shape((1, ny, nz), F32),
        shape(tiles, F32),
        shape((1, 2, 2, slots), F32),
    )
    results = pl.pallas_call(
        run,
        out_shape=shapes,
        in_specs=[in_hbm] * 2 + [in_vmem] * 11,
        out_specs=(in_vmem,) * 3,
        scratch_shapes=[
            pltpu.SMEM((1, 2), I32),
            vmem((ny, nz), I32),
            vmem((ny, nz), F32),
            vmem(both, F32),
            vmem((STEPS, 2, ny, nz), F32),
            vmem(tiles, F32),
            vmem((2, 2, 1, slots), F32),
            vmem((2, 2, slots), F32),
            vmem((2, 2, 1, slots), F32),
            vmem((2, 2, slots), F32),
            vmem((STEPS, ny, nz), F32),
            vmem(tiles, F32),
            vmem((chunks - early, nz, CHUNK), BF16),
            vmem((chunks - early, CHUNK, nz), BF16),
            vmem((chunks - early, ny, CHUNK), BF16),
            vmem((2 * ny, nz), BF16),
            vmem((chunks, ROWS, LANES), F32),
            vmem((chunks, 2, ROWS, LANES), F32),
            vmem((subs, ROWS, LANES), F32),
            vmem((2, 2, LANES, slots), BF16),
            vmem((2, 2, half * ROWS, slots), F32),
            dma((2,)),
            dma((11,)),
            dma((11,)),
        ],
        compiler_params=params(1),
        name="run",
    )(*kept(migrant_count, inlet_mask), *close(met))
    field, size_out, arrivals = pl.pallas_call(
        store,
        out_shape=shapes,
        in_specs=[anywhere] * 3,
        out_specs=(in_hbm,) * 3,
        scratch_shapes=[dma((3,))],
        name="store",
    )(*close(results))
    return (field, size_out.reshape(parcels), arrivals)


def solution(mesh):
    rows = P(("slab", "grp"))
    return jax.shard_map(
        local,
        mesh=mesh,
        in_specs=(rows,) * 10,
        out_specs=(rows,) * 3,
        check_vma=False,
    )
```

```python
import jax
import jax.numpy as jnp
from jax import lax
from jax.experimental import pallas as pl
from jax.experimental.pallas import tpu as pltpu
from jax.sharding import PartitionSpec as P

STEPS = 2
SUBS = 2
GROWTH = 0.08
VOLUME = 1.0
NUCLEATE = 0.02
DIFFUSE = 0.12
INLET = 4.0

LANES = 128
ROWS = 8
CHUNK = ROWS * LANES
EARLY = 1
LAG = 2
BLOCK = 4
LANE_CHUNKS = 3
MESH = pl.DeviceIdType.MESH
F32 = jnp.float32
BF16 = jnp.bfloat16
I32 = jnp.int32


def softplus(x):
    return jnp.maximum(x, 0.0) + jnp.log1p(jnp.exp(-jnp.abs(x)))


def pieces(x, count):
    out = []
    for _ in range(count):
        top = x.astype(BF16)
        out.append(top)
        x = x - top.astype(F32)
    return out


def when(condition, action):
    if condition is None:
        action()
    else:
        pl.when(condition)(action)


def greet(peer):
    barrier = pltpu.get_barrier_semaphore()
    pl.semaphore_signal(barrier, inc=1, device_id=peer, device_id_type=MESH)


class Hot:
    def __init__(self, base, ny, nz):
        self.base, self.ny, self.nz = base, ny, nz
        self.shift = nz.bit_length() - 1
        self.chunks = {}
        self.by_lane = {}

    def add(self, first, refs):
        for index in range(refs[0].shape[0]):
            self.chunks[first + index] = (*refs, index)

    def build(self, chunk, tile):
        hot_p, hot_t, hot_l, at = self.chunks[chunk]
        cell = tile - self.base
        place = cell & (self.nz - 1)
        line = cell >> self.shift
        placed, lined = place.astype(F32), line.astype(F32)
        turned = jnp.transpose(placed)

        def iota(shape, dim):
            return lax.broadcasted_iota(I32, shape, dim).astype(F32).astype(BF16)

        down_nz = iota((self.nz, LANES), 0)
        down_ny = iota((self.ny, LANES), 0)
        along_nz = iota((LANES, self.nz), 1)
        one, none = jnp.ones((), BF16), jnp.zeros((), BF16)
        for j in range(ROWS):
            columns = pl.ds(LANES * j, LANES)

            def spread(row, shape):
                return jnp.broadcast_to(row, shape).astype(BF16)

            row = slice(j, j + 1)
            if chunk not in self.by_lane:
                hot_p[at, :, columns] = jnp.where(
                    down_nz == spread(placed[row, :], down_nz.shape), one, none
                )
            hot_l[at, :, columns] = jnp.where(
                down_ny == spread(lined[row, :], down_ny.shape), one, none
            )
            hot_t[at, columns, :] = jnp.where(
                along_nz == spread(turned[:, row], along_nz.shape), one, none
            )

    def here(self, cells):
        line = (cells - self.base) >> self.shift
        return jnp.logical_and(line >= 0, line < self.ny)

    def gather(self, chunk, table, pair, local):
        if chunk in self.by_lane:
            local[chunk] = self.gather_lanes(self.by_lane[chunk]() - self.base, table)
            return
        hot_p, _, hot_l, at = self.chunks[chunk]
        ny = self.ny
        both = jnp.dot(pair[...], hot_p[at], preferred_element_type=F32)
        read = (both[:ny] + both[ny:]) * hot_l[at].astype(F32)
        flat = jnp.sum(read, axis=0, keepdims=True)
        for j in range(ROWS):
            local[chunk, pl.ds(j, 1), :] = flat[:, LANES * j : LANES * (j + 1)]

    def gather_lanes(self, cell, table):
        place = cell & (LANES - 1)
        row_of = cell >> (LANES.bit_length() - 1)
        across = self.nz // LANES
        found = [jnp.zeros((ROWS, LANES), F32) for _ in range(2)]
        for row in range(self.ny * across):
            columns = pl.ds(LANES * (row % across), LANES)
            line = table[pl.ds(row // across, 1), columns]
            read = jnp.take_along_axis(
                jnp.broadcast_to(line, (ROWS, LANES)),
                place,
                axis=1,
                mode="promise_in_bounds",
            )
            found[row % 2] = jnp.where(row_of == row, read, found[row % 2])
        return found[0] + found[1]

    def scatter(self, chunk, mass):
        _, hot_t, hot_l, at = self.chunks[chunk]
        lines = hot_l[at]
        tops, rests = [], []
        for j in range(ROWS):
            block = lines[:, LANES * j : LANES * (j + 1)]
            row = (self.ny, LANES)
            top = jnp.broadcast_to(mass[chunk, 0, pl.ds(j, 1), :], row)
            rest = jnp.broadcast_to(mass[chunk, 1, pl.ds(j, 1), :], row)
            tops.append(block * top.astype(BF16))
            rests.append(block * rest.astype(BF16))
        left = jnp.concatenate(
            [jnp.concatenate(tops, axis=1), jnp.concatenate(rests, axis=1)], axis=0
        )
        return jnp.dot(left, hot_t[at], preferred_element_type=F32)


def set_mass(mass, chunk, value):
    top = value.astype(BF16).astype(F32)
    mass[chunk, 0] = top
    mass[chunk, 1] = value - top


def in_turn(hot, chunks):
    by_lane = [c for c in chunks if c in hot.by_lane]
    others = [c for c in chunks if c not in hot.by_lane]
    out = []
    while by_lane or others:
        out += others[:1] + by_lane[:1]
        others, by_lane = others[1:], by_lane[1:]
    return out


def deposit(chunks, total, hot, table, pair, local, mass, weigh):
    chunks = in_turn(hot, chunks)
    for k in range(len(chunks) + LAG):
        if k < len(chunks):
            hot.gather(chunks[k], table, pair, local)
            weigh(chunks[k])
        if k >= LAG:
            total = total + hot.scatter(chunks[k - LAG], mass)
    return total


def split(plane, table, pair):
    ny = plane.shape[0]
    table[...] = plane
    top, rest = pieces(plane, 2)
    pair[pl.ds(0, ny), :] = top
    pair[pl.ds(ny, ny), :] = rest


def grower(hot, cells, sizes, weights, local, mass):
    def grow(chunk):
        here = jnp.where(hot.here(cells[chunk]), 1.0, 0.0)
        size = sizes[chunk]
        grown = size + here * GROWTH * softplus(local[chunk] - 1.0)
        sizes[chunk] = grown
        cubes = grown * grown * grown - size * size * size
        set_mass(mass, chunk, here * weights[chunk] * VOLUME * cubes)

    return grow


def event_tiles(sub, ncell, ncount):
    rows = ROWS // 2
    cell, count = [], []
    for side in range(2):
        for j in range(rows):
            columns = slice(LANES * j, LANES * (j + 1))
            cell.append(ncell[side, sub : sub + 1, columns])
            count.append(ncount[side, sub : sub + 1, columns])
    return jnp.concatenate(cell, axis=0), jnp.concatenate(count, axis=0).astype(F32)


def read_by_lane(hot, cells, ncell, ncount):
    parcel_chunks = cells.shape[0]
    for chunk in range(parcel_chunks):
        if chunk % BLOCK >= BLOCK - LANE_CHUNKS:
            hot.by_lane[chunk] = lambda chunk=chunk: cells[chunk]
    for sub in range(STEPS * SUBS):
        hot.by_lane[parcel_chunks + sub] = lambda sub=sub: event_tiles(
            sub, ncell, ncount
        )[0]


def meet(
    live_ref,
    sat_hbm,
    size_hbm,
    weight_hbm,
    cell_hbm,
    ncell_hbm,
    ncount_hbm,
    mrows_hbm,
    field,
    sizes,
    weights,
    cells,
    ncell,
    ncount,
    mrows,
    total,
    hot_p,
    hot_t,
    hot_l,
    cells_in,
    got_cells,
    got_sizes,
    got_weights,
    got_ncell,
    got_ncount,
    got_mrows,
    table,
    pair,
    local,
    mass,
    local_sem,
    send_sem,
    recv_sem,
):
    ny, nz = field.shape
    half = cells_in.shape[0]
    s = lax.axis_index("slab")
    g = lax.axis_index("grp")
    partner = (s, 1 - g)
    greet(partner)
    mine = pl.ds(0, half)
    loads = []
    for index, (source, target) in enumerate(
        (
            (cell_hbm, cells_in),
            (sat_hbm.at[0], field),
            (size_hbm, sizes.at[mine]),
            (weight_hbm, weights.at[mine]),
            (ncell_hbm.at[0], ncell.at[0]),
            (ncount_hbm.at[0], ncount.at[0]),
            (mrows_hbm.at[0], mrows.at[0]),
        )
    ):
        copy = pltpu.make_async_copy(source, target, local_sem.at[index])
        copy.start()
        loads.append(copy)

    loads[0].wait()
    live = live_ref[0]
    tiles = cells_in.shape
    row_of = (
        lax.broadcasted_iota(I32, tiles, 0) * CHUNK
        + lax.broadcasted_iota(I32, tiles, 1) * LANES
        + lax.broadcasted_iota(I32, tiles, 2)
    )
    own_cells = jnp.where(row_of < live, cells_in[...], -1)
    cells_in[...] = own_cells
    cells[mine] = own_cells

    pl.semaphore_wait(pltpu.get_barrier_semaphore(), 1)
    entry = []
    for index, (source, target) in enumerate(
        (
            (cells_in, got_cells),
            (ncell_hbm.at[0], got_ncell),
            (size_hbm, got_sizes),
            (weight_hbm, got_weights),
            (ncount_hbm.at[0], got_ncount),
            (mrows_hbm.at[0], got_mrows),
        )
    ):
        copy = pltpu.make_async_remote_copy(
            src_ref=source,
            dst_ref=target,
            send_sem=send_sem.at[index],
            recv_sem=recv_sem.at[index],
            device_id=partner,
            device_id_type=MESH,
        )
        copy.start()
        entry.append(copy)

    hot = Hot(g * (ny * nz), ny, nz)
    hot.add(0, (hot_p, hot_t, hot_l))
    read_by_lane(hot, cells, ncell, ncount)
    for chunk in range(half):
        hot.build(chunk, cells[chunk])
    for copy in loads[1:]:
        copy.wait()
    split(field[...], table, pair)
    grow = grower(hot, cells, sizes, weights, local, mass)
    zero = jnp.zeros((2 * ny, nz), F32)
    total[...] = deposit(list(range(half)), zero, hot, table, pair, local, mass, grow)

    theirs = pl.ds(half, half)
    entry[0].wait_recv()
    cells[theirs] = got_cells[...]
    for chunk in range(half, 2 * half):
        hot.build(chunk, cells[chunk])
    entry[1].wait_recv()
    ncell[1] = got_ncell[...]
    for copy in entry[2:]:
        copy.wait_recv()
    sizes[theirs] = got_sizes[...]
    weights[theirs] = got_weights[...]
    ncount[1] = got_ncount[...]
    mrows[1] = got_mrows[...]
    for sub in range(SUBS):
        hot.build(2 * half + sub, event_tiles(sub, ncell, ncount)[0])
    for copy in entry:
        copy.wait_send()


def run(
    mcount_hbm,
    inlet_hbm,
    field_in,
    sizes_in,
    weights,
    cells,
    ncell,
    ncount,
    mrows,
    total_in,
    hot_p,
    hot_t,
    hot_l,
    field_ref,
    size_ref,
    arrive_ref,
    mcount_ref,
    inlet,
    field,
    sizes,
    halo,
    back,
    mig_size,
    mig_weight,
    got_size,
    got_weight,
    plane_out,
    size_send,
    late_p,
    late_t,
    late_l,
    table,
    pair,
    local,
    mass,
    evcount,
    mig_hot,
    mig_line,
    local_sem,
    send_sem,
    recv_sem,
):
    ny, nz = field.shape
    half = back.shape[0]
    parcel_chunks = 2 * half
    s = lax.axis_index("slab")
    g = lax.axis_index("grp")
    slabs = lax.axis_size("slab")
    has_down = s > 0
    has_up = s < slabs - 1
    partner = (s, 1 - g)
    other = (s + 2 * g - 1, 1 - g)
    has_other = jnp.logical_or(
        jnp.logical_and(g == 0, has_down), jnp.logical_and(g == 1, has_up)
    )

    def greet_slab(slab):
        greet((slab, g))
        greet((slab, 1 - g))

    pl.when(has_down)(lambda: greet_slab(s - 1))
    pl.when(has_up)(lambda: greet_slab(s + 1))
    greet(partner)
    loads = []
    for index, (source, target) in enumerate(
        ((mcount_hbm.at[0], mcount_ref.at[0]), (inlet_hbm.at[0], inlet))
    ):
        copy = pltpu.make_async_copy(source, target, local_sem.at[index])
        copy.start()
        loads.append(copy)

    def remote(index, source, target, peer, sends=None):
        copy = pltpu.make_async_remote_copy(
            src_ref=source,
            dst_ref=target,
            send_sem=send_sem.at[index],
            recv_sem=recv_sem.at[index],
            device_id=peer,
            device_id_type=MESH,
        )
        when(sends, copy.start)
        return copy

    hot = Hot(g * (ny * nz), ny, nz)
    hot.add(0, (hot_p, hot_t, hot_l))
    hot.add(hot_p.shape[0], (late_p, late_t, late_l))
    read_by_lane(hot, cells, ncell, ncount)
    sizes[...] = sizes_in[...]
    grow = grower(hot, cells, sizes, weights, local, mass)

    def weigh(chunk):
        if chunk < parcel_chunks:
            grow(chunk)
        else:
            made = evcount[chunk - parcel_chunks]
            set_mass(mass, chunk, made * NUCLEATE * softplus(local[chunk] - 1.0))

    for sub in range(STEPS * SUBS):
        evcount[sub] = event_tiles(sub, ncell, ncount)[1]

    def substep(plane, chunks, total):
        split(plane, table, pair)
        total = deposit(chunks, total, hot, table, pair, local, mass, weigh)
        field[...] = plane - (total[:ny] + total[ny:])

    lane = lax.broadcasted_iota(I32, (ny, nz), 1)
    line = lax.broadcasted_iota(I32, (ny, nz), 0)

    def mix(step):
        plane_out[step] = field[...]
        source = plane_out.at[step]
        first = remote(2 * step, source, halo.at[step, 0], partner)
        second = remote(2 * step + 1, source, halo.at[step, 1], other, has_other)
        return ((first, None), (second, has_other))

    def mixed(step, copies):
        plane = field[...]
        beside = jnp.where(line == 0, 0.0, pltpu.roll(plane, 1, 0))
        beside = beside + jnp.where(line == ny - 1, 0.0, pltpu.roll(plane, ny - 1, 0))
        beside = beside + jnp.where(lane == 0, 0.0, pltpu.roll(plane, 1, 1))
        beside = beside + jnp.where(lane == nz - 1, 0.0, pltpu.roll(plane, nz - 1, 1))
        for copy, condition in copies:
            when(condition, copy.wait_recv)
        beside = beside + halo[step, 0] + halo[step, 1]
        plane = plane + DIFFUSE * (beside - 6.0 * plane)
        return plane + inlet[...].astype(F32) * (INLET - plane)

    @pl.when(jnp.logical_not(has_other))
    def _():
        for step in range(STEPS):
            halo[step, 1] = jnp.zeros((ny, nz), F32)

    def clear(index):
        got_size[index] = jnp.zeros(got_size.shape[1:], F32)
        got_weight[index] = jnp.zeros(got_weight.shape[1:], F32)

    pl.when(jnp.logical_not(has_down))(lambda: clear(0))
    pl.when(jnp.logical_not(has_up))(lambda: clear(1))

    every = list(range(parcel_chunks))
    zero = jnp.zeros((2 * ny, nz), F32)
    substep(field_in[...], every[half:] + [parcel_chunks], total_in[...])
    substep(field[...], every + [parcel_chunks + 1], zero)
    for copy in loads:
        copy.wait()
    pl.semaphore_wait(
        pltpu.get_barrier_semaphore(),
        1 + 2 * has_down.astype(I32) + 2 * has_up.astype(I32),
    )
    planes = mix(0)
    slots = mrows.shape[2]
    rows_of = half * ROWS
    down_lanes = lax.broadcasted_iota(I32, (LANES, slots), 0)
    down_rows = lax.broadcasted_iota(I32, (rows_of, slots), 0)
    slot = lax.broadcasted_iota(I32, (1, slots), 1)
    for side in range(2):
        for j in range(2):
            rows = mrows[side, pl.ds(j, 1), :]
            mig_hot[side, j] = jnp.where(
                down_lanes == (rows & (LANES - 1)), 1.0, 0.0
            ).astype(BF16)
            mig_line[side, j] = jnp.where(down_rows == (rows >> 7), 1.0, 0.0)

    def pick(side, j, flat):
        both = jnp.dot(flat, mig_hot[side, j], preferred_element_type=F32)
        read = sum(
            both[at : at + rows_of] for at in range(0, flat.shape[0], rows_of)
        )
        return jnp.sum(read * mig_line[side, j], axis=0, keepdims=True)

    def flat_pieces(table, count):
        return jnp.concatenate(pieces(table.reshape(rows_of, LANES), count), axis=0)

    flat = flat_pieces(weights[pl.ds(0, half)], 3)
    for j in range(2):
        used = jnp.where(slot < mcount_ref[0, j], 1.0, 0.0)
        mig_weight[j, pl.ds(0, 1), :] = used
        mig_weight[j, pl.ds(1, 1), :] = pick(0, j, flat) * used
    last = []

    def send_both(index, source, target, grp):
        low = remote(index, source[0], target[1], (s - 1, grp), has_down)
        high = remote(index + 1, source[1], target[0], (s + 1, grp), has_up)
        last.append((low, has_down, has_up))
        last.append((high, has_up, has_down))

    send_both(
        4,
        (mig_weight.at[0], mig_weight.at[1]),
        (got_weight.at[0], got_weight.at[1]),
        g,
    )
    for sub in range(SUBS, STEPS * SUBS):
        hot.build(parcel_chunks + sub, event_tiles(sub, ncell, ncount)[0])
    substep(mixed(0, planes), every + [parcel_chunks + 2], zero)
    plane = field[...]
    split(plane, table, pair)
    events = parcel_chunks + 3
    total = zero
    waiting = []
    for chunk in in_turn(hot, every + [events]):
        hot.gather(chunk, table, pair, local)
        weigh(chunk)
        waiting.append(chunk)
        if len(waiting) > LAG:
            total = total + hot.scatter(waiting.pop(0), mass)
    for side in range(2):
        at = pl.ds(side * half, half)
        flat = flat_pieces(jnp.where(hot.here(cells[at]), sizes[at], 0.0), 2)
        for j in range(2):
            mig_size[side, j] = pick(side, j, flat)
    for chunk in waiting[:EARLY]:
        total = total + hot.scatter(chunk, mass)
    for side in range(2):
        send_both(
            7 + 2 * side,
            (mig_size.at[side, 0], mig_size.at[side, 1]),
            (got_size.at[0, side], got_size.at[1, side]),
            g if side == 0 else 1 - g,
        )
    for chunk in waiting[EARLY:]:
        total = total + hot.scatter(chunk, mass)
    field[...] = plane - (total[:ny] + total[ny:])
    planes = planes + mix(1)
    theirs = pl.ds(half, half)
    size_send[...] = sizes[theirs]
    sent_back = remote(6, size_send, back, partner)
    sent_back.wait_recv()
    mine = pl.ds(0, half)
    final = jnp.where(hot.here(cells[mine]), sizes[mine], back[...])
    size_ref[...] = jnp.where(cells[mine] >= 0, final, 0.0)
    field_ref[0] = mixed(1, planes[2:])
    for copy, _, receives in last:
        when(receives, copy.wait_recv)
    for side in range(2):
        used = got_weight[side, pl.ds(0, 1), :]
        size = got_size[side, 0] + got_size[side, 1]
        arrive_ref[0, side, pl.ds(0, 1), :] = size * used
        arrive_ref[0, side, pl.ds(1, 1), :] = got_weight[side, pl.ds(1, 1), :]
    sent_back.wait_send()
    for copy, sends in planes:
        when(sends, copy.wait_send)
    for copy, sends, _ in last:
        when(sends, copy.wait_send)


def store(field_ref, size_ref, arrive_ref, field_out, size_out, arrive_out, sem):
    copies = [
        pltpu.make_async_copy(source, target, sem.at[index])
        for index, (source, target) in enumerate(
            ((field_ref, field_out), (size_ref, size_out), (arrive_ref, arrive_out))
        )
    ]
    for copy in copies:
        copy.start()
    for copy in copies:
        copy.wait()


def local(
    saturation,
    inlet_mask,
    crystal_size,
    crystal_weight,
    crystal_cell,
    live_count,
    nucleus_cell,
    nucleus_count,
    migrant_rows,
    migrant_count,
):
    _, ny, nz = saturation.shape
    parcels = crystal_size.shape[0]
    half = parcels // CHUNK
    subs, events = nucleus_cell.shape[1:]
    slots = migrant_rows.shape[2]
    tiles = (half, ROWS, LANES)
    both = (2 * half, ROWS, LANES)
    chunks = 2 * half + subs
    early = 2 * half + SUBS
    vmem = pltpu.VMEM
    dma = pltpu.SemaphoreType.DMA
    in_smem = pl.BlockSpec(memory_space=pltpu.SMEM)
    in_vmem = pl.BlockSpec(memory_space=vmem)
    in_hbm = pl.BlockSpec(memory_space=pltpu.HBM)
    anywhere = pl.BlockSpec(memory_space=pl.ANY)

    def kept(*arrays):
        return [pltpu.with_memory_space_constraint(a, pltpu.HBM) for a in arrays]

    def close(arrays):
        return [pltpu.with_memory_space_constraint(a, vmem) for a in arrays]

    def params(index):
        return pltpu.CompilerParams(
            collective_id=index,
            has_side_effects=True,
            vmem_limit_bytes=20 * 1024 * 1024,
        )

    shape = jax.ShapeDtypeStruct
    met = pl.pallas_call(
        meet,
        out_shape=(
            shape((ny, nz), F32),
            shape(both, F32),
            shape(both, F32),
            shape(both, I32),
            shape((2, subs, events), I32),
            shape((2, subs, events), I32),
            shape((2, 2, slots), I32),
            shape((2 * ny, nz), F32),
            shape((early, nz, CHUNK), BF16),
            shape((early, CHUNK, nz), BF16),
            shape((early, ny, CHUNK), BF16),
        ),
        in_specs=[in_smem] + [in_hbm] * 7,
        out_specs=(in_vmem,) * 11,
        scratch_shapes=[
            vmem(tiles, I32),
            vmem(tiles, I32),
            vmem(tiles, F32),
            vmem(tiles, F32),
            vmem((subs, events), I32),
            vmem((subs, events), I32),
            vmem((2, slots), I32),
            vmem((ny, nz), F32),
            vmem((2 * ny, nz), BF16),
            vmem((chunks, ROWS, LANES), F32),
            vmem((chunks, 2, ROWS, LANES), F32),
            dma((7,)),
            dma((6,)),
            dma((6,)),
        ],
        compiler_params=params(0),
        name="meet",
    )(
        live_count,
        *kept(
            saturation,
            crystal_size.reshape(tiles),
            crystal_weight.reshape(tiles),
            crystal_cell.reshape(tiles),
            nucleus_cell,
            nucleus_count,
            migrant_rows,
        ),
    )
    shapes = (
        shape((1, ny, nz), F32),
        shape(tiles, F32),
        shape((1, 2, 2, slots), F32),
    )
    results = pl.pallas_call(
        run,
        out_shape=shapes,
        in_specs=[in_hbm] * 2 + [in_vmem] * 11,
        out_specs=(in_vmem,) * 3,
        scratch_shapes=[
            pltpu.SMEM((1, 2), I32),
            vmem((ny, nz), I32),
            vmem((ny, nz), F32),
            vmem(both, F32),
            vmem((STEPS, 2, ny, nz), F32),
            vmem(tiles, F32),
            vmem((2, 2, 1, slots), F32),
            vmem((2, 2, slots), F32),
            vmem((2, 2, 1, slots), F32),
            vmem((2, 2, slots), F32),
            vmem((STEPS, ny, nz), F32),
            vmem(tiles, F32),
            vmem((chunks - early, nz, CHUNK), BF16),
            vmem((chunks - early, CHUNK, nz), BF16),
            vmem((chunks - early, ny, CHUNK), BF16),
            vmem((ny, nz), F32),
            vmem((2 * ny, nz), BF16),
            vmem((chunks, ROWS, LANES), F32),
            vmem((chunks, 2, ROWS, LANES), F32),
            vmem((subs, ROWS, LANES), F32),
            vmem((2, 2, LANES, slots), BF16),
            vmem((2, 2, half * ROWS, slots), F32),
            dma((2,)),
            dma((11,)),
            dma((11,)),
        ],
        compiler_params=params(1),
        name="run",
    )(*kept(migrant_count, inlet_mask), *close(met))
    field, size_out, arrivals = pl.pallas_call(
        store,
        out_shape=shapes,
        in_specs=[anywhere] * 3,
        out_specs=(in_hbm,) * 3,
        scratch_shapes=[dma((3,))],
        name="store",
    )(*close(results))
    return (field, size_out.reshape(parcels), arrivals)


def solution(mesh):
    rows = P(("slab", "grp"))
    return jax.shard_map(
        local,
        mesh=mesh,
        in_specs=(rows,) * 10,
        out_specs=(rows,) * 3,
        check_vma=False,
    )
```
